512 devices in a mesh: tile: 32 (over z_lo, y, core), date: 16 (over z_hi, x).
Axes of the slice: x: 4, y: 4, z: 16 (z_hi: 4, z_lo: 4; z = z_hi * 4 + z_lo), core: 2. Of those that a mesh axis runs over, the one named last changes fastest.
Arguments:
- secondary: bfloat16 [16, 2, 3072, 1024], P('date', None, 'tile'), may hold values from -6 to 6
- primary: bfloat16 [2, 3072, 1024], P(None, 'tile', 'date'), may hold values from -6 to 6
- margin_mask: int32 [3072], P('tile'), may hold values from 0 to 1, as said below
- az_off: int32 [16, 32], P('date', 'tile'), may hold values from -16 to 16
- rg_off: int32 [16, 32], P('date', 'tile'), may hold values from -16 to 16
- az_frac: float32 [16, 32], P('date', 'tile'), may hold values from 0 to 1
- rg_frac: float32 [16, 32], P('date', 'tile'), may hold values from 0 to 1
Outputs:
- looks: float32 [16, 2, 1536, 128], P('date', None, 'tile')
The draws below stay inside these ranges and needn't reach their ends.
Inputs may be any that keep to these rules, and one draw needn't show every extreme that they name: `margin_mask`: ones lie only in the last 64 rows of each tile of 96 rows, and the last row of every tile is 1.
All inputs are finite; a program needn't handle non-finite values.
Results may differ from the reference program's by a relative error of at most 0.017.
Values may be sent and summed in bfloat16 or wider, within the bound.
A program may use at most 64 MiB of HBM per device.

```python
import jax
import jax.numpy as jnp
from jax import lax

ROWS = 3072
COLS = 1024
KA = 16
KR = 16
LAG = 64
LA = 2
LR = 8
DATES = 16
TILES = 32
ROW_DEV = 96


def draw_margin_mask(key, part):
    random_bits = jax.random.randint(jax.random.fold_in(key, 11), (ROWS,), 0, 2)
    position = jnp.arange(ROWS, dtype=jnp.int32) % ROW_DEV
    near_end = position >= ROW_DEV - LAG
    last_row = position == ROW_DEV - 1
    chosen = near_end & ((random_bits == 1) | last_row)
    return jnp.where(chosen, 1, 0).astype(jnp.int32)


def plant(values, stream_key, smallest, top_value):
    spot = [jax.random.randint(jax.random.fold_in(stream_key, axis), (), 0, length) for axis, length in enumerate(values.shape)]
    widest = values.shape.index(max(values.shape))
    beside = spot[:widest] + [(spot[widest] + 1) % values.shape[widest]] + spot[widest + 1:]
    return values.at[tuple(spot)].set(smallest).at[tuple(beside)].set(top_value)


def levels(stream_key, extent, cuts, low, largest):
    gain, own = 1.0, jax.random.fold_in(stream_key, 6)
    for axis_at, shards_of in cuts:
        steps = jnp.exp(jax.random.uniform(jax.random.fold_in(own, axis_at), (shards_of,), jnp.float32, low / len(cuts), largest / len(cuts)))
        gain = gain * jnp.repeat(steps, extent[axis_at] // shards_of).reshape([-1 if axis == axis_at else 1 for axis in range(len(extent))])
    return gain


def centred(own_key, extent, deviation, most, shards=(), held_as=jnp.bfloat16):
    level = levels(own_key, extent, shards, -0.22, 0.18) if shards else 1.0
    result = jax.random.normal(own_key, extent, jnp.float32) * deviation * level
    return jnp.minimum(jnp.maximum(result, -most), most).astype(held_as)


def setup_inputs(seed: int = 0) -> dict:
    arg_keys = jax.random.split(jax.random.key(seed), 8)
    return {
        "secondary": centred(arg_keys[0], (DATES, 2, ROWS, COLS), 1.0, 6.0, ((0, 16), (2, 32))),
        "primary": centred(arg_keys[1], (2, ROWS, COLS), 1.0, 6.0, ((1, 32), (2, 16))),
        "margin_mask": draw_margin_mask(jax.random.fold_in(arg_keys[7], 71), 0),
        "az_off": plant(jax.random.randint(arg_keys[3], (DATES, TILES), -KA, KA + 1), jax.random.fold_in(arg_keys[3], 1), -KA, KA).astype(jnp.int32),
        "rg_off": plant(jax.random.randint(arg_keys[4], (DATES, TILES), -KR, KR + 1), jax.random.fold_in(arg_keys[4], 1), -KR, KR).astype(jnp.int32),
        "az_frac": jnp.clip(1.0 * jax.random.uniform(arg_keys[5], (DATES, TILES), jnp.float32) ** levels(arg_keys[5], (DATES, TILES), ((0, 16), (1, 32)), -0.2, 0.2), 0.0, 1.0),
        "rg_frac": jnp.clip(1.0 * jax.random.uniform(arg_keys[6], (DATES, TILES), jnp.float32) ** levels(arg_keys[6], (DATES, TILES), ((0, 16), (1, 32)), -0.2, 0.2), 0.0, 1.0),
    }


def window(dist):
    return jnp.sinc(dist) * (0.5 + 0.5 * jnp.cos(jnp.pi * dist / 4.0))

def reference(secondary, primary, margin_mask, az_off, rg_off, az_frac, rg_frac):
    rim_rows = KA + 4
    rim_cols = KR + 4
    prim = primary.astype(jnp.float32)
    weight = margin_mask.astype(jnp.float32)[:, None]
    count = jnp.sum(margin_mask.astype(jnp.float32)) * COLS

    def one_date(items):
        image, a_row, r_row, fa_row, fr_row = items
        padded = jnp.pad(image, ((0, 0), (rim_rows, rim_rows), (0, 0)))

        def tile_az(tile_id, shift, frac):
            block = lax.dynamic_slice_in_dim(padded, (tile_id * ROW_DEV).astype(jnp.int32), ROW_DEV + 2 * rim_rows, axis=1)
            total = jnp.zeros((2, ROW_DEV, COLS), jnp.float32)
            for step in range(8):
                offset = step - 3
                coeff = window(jnp.float32(offset) - frac).astype(jnp.bfloat16).astype(jnp.float32)
                piece = lax.dynamic_slice_in_dim(block, (shift + rim_rows + offset).astype(jnp.int32), ROW_DEV, axis=1)
                total = total + coeff * piece.astype(jnp.float32)
            return total.astype(jnp.bfloat16)
        azim = jax.vmap(tile_az)(jnp.arange(TILES, dtype=jnp.int32), a_row, fa_row)
        cpad = jnp.pad(azim, ((0, 0), (0, 0), (0, 0), (rim_cols, rim_cols)))

        def tile_rg(block, shift, frac):
            total = jnp.zeros((2, ROW_DEV, COLS), jnp.float32)
            for step in range(8):
                offset = step - 3
                coeff = window(jnp.float32(offset) - frac).astype(jnp.bfloat16).astype(jnp.float32)
                piece = lax.dynamic_slice_in_dim(block, (shift + rim_cols + offset).astype(jnp.int32), COLS, axis=2)
                total = total + coeff * piece.astype(jnp.float32)
            return total.astype(jnp.bfloat16)
        resampled = jax.vmap(tile_rg)(cpad, r_row, fr_row)
        resampled = resampled.transpose(1, 0, 2, 3).reshape(2, ROWS, COLS).astype(jnp.float32)
        ifg_re = prim[0] * resampled[0] + prim[1] * resampled[1]
        ifg_im = prim[1] * resampled[0] - prim[0] * resampled[1]
        tail = jnp.zeros((LAG, COLS), jnp.float32)
        l_re = jnp.concatenate([ifg_re[LAG:], tail], axis=0)
        l_im = jnp.concatenate([ifg_im[LAG:], tail], axis=0)
        e_re = jnp.sum(weight * (ifg_re * l_re + ifg_im * l_im))
        e_im = jnp.sum(weight * (ifg_im * l_re - ifg_re * l_im))
        power = jnp.sum(weight * 0.5 * (ifg_re * ifg_re + ifg_im * ifg_im + l_re * l_re + l_im * l_im))
        magnitude = jnp.sqrt(e_re * e_re + e_im * e_im)
        floor_val = (power + 1e-06) / jnp.sqrt(jnp.maximum(count, 1.0))
        denom = jnp.maximum(magnitude, floor_val)
        u_re = e_re / denom
        u_im = e_im / denom
        c_re = ifg_re * u_re + ifg_im * u_im
        c_im = ifg_im * u_re - ifg_re * u_im
        both = jnp.stack([c_re, c_im], axis=0)
        return both.reshape(2, ROWS // LA, LA, COLS // LR, LR).mean(axis=(2, 4))
    return lax.map(one_date, (secondary, az_off, rg_off, az_frac, rg_frac))
```

```python
import functools

import jax
import jax.numpy as jnp
from jax import lax
from jax.experimental import pallas as pl
from jax.experimental.pallas import tpu as pltpu
from jax.sharding import PartitionSpec as P

LAG = 64
LA = 2
LR = 8
NX = 4
RIM = 32
SIDE = 128
BLOCK = 256
MESH = pl.DeviceIdType.MESH
F32 = jnp.float32
BF16 = jnp.bfloat16


def iota(shape, dim):
    return lax.broadcasted_iota(jnp.int32, shape, dim)


def tap_rows(frac, lanes):
    dist = iota((8, lanes), 0).astype(F32) - 3.0 - frac
    arg = jnp.pi * dist
    sinc = jnp.where(dist == 0.0, 1.0, jnp.sin(arg) / jnp.where(dist == 0.0, 1.0, arg))
    return sinc * (0.5 + 0.5 * jnp.cos(arg * 0.25))


def band(rows, first):
    total = jnp.zeros(first.shape, F32)
    for j in range(8):
        total = jnp.where(first == j - 3, rows[j : j + 1], total)
    return total.astype(BF16)


def kernel(
    tiles, dates,
    sec, prim, mask, az_off, rg_off, az_frac, rg_frac,
    out,
    ext, prim_in, azim, gath, res, ifg, lag_out, lag_in, stat_out, stat_in, acc,
    local_sem, halo_send, halo_recv, z_send, z_recv, x_send, x_recv,
    lag_send, lag_recv, stat_send, stat_recv,
):
    nz = dates // NX
    rows_n = sec.shape[2]
    cols_n = sec.shape[3]
    width = prim.shape[2]
    chunks = cols_n // 128
    t = lax.axis_index("tile")
    d = lax.axis_index("date")
    zh, x = d // NX, lax.rem(d, NX)
    step = 1 - 2 * lax.rem(t, 2)

    def z_at(k):
        return lax.rem(zh + k * step + 2 * nz, nz)

    def date_at(z, xx):
        return z * NX + xx

    def remote(src, dst, ss, rs, tile, date):
        return pltpu.make_async_remote_copy(
            src_ref=src, dst_ref=dst, send_sem=ss, recv_sem=rs,
            device_id={"tile": tile, "date": date}, device_id_type=MESH,
        )

    barrier = pltpu.get_barrier_semaphore()
    partners = 0
    for k in range(1, NX):
        pl.semaphore_signal(barrier, inc=1, device_id={"tile": t, "date": date_at(zh, lax.rem(x + k, NX))}, device_id_type=MESH)
        partners += 1
    for k in (1, -1):
        pl.semaphore_signal(barrier, inc=1, device_id={"tile": t, "date": date_at(z_at(k), x)}, device_id_type=MESH)
        partners += 1
    for k in range(1, tiles):
        pl.semaphore_signal(barrier, inc=1, device_id={"tile": lax.rem(t + k, tiles), "date": d}, device_id_type=MESH)
        partners += 1

    prim_copy = pltpu.make_async_copy(prim, prim_in, local_sem.at[0])
    prim_copy.start()
    own_copy = pltpu.make_async_copy(sec.at[0], ext.at[:, pl.ds(RIM, rows_n), :], local_sem.at[1])
    own_copy.start()

    @pl.when(t == 0)
    def _():
        ext[:, pl.ds(0, RIM), :] = jnp.zeros((2, RIM, cols_n), BF16)

    @pl.when(t == tiles - 1)
    def _():
        ext[:, pl.ds(RIM + rows_n, RIM), :] = jnp.zeros((2, RIM, cols_n), BF16)
        lag_in[...] = jnp.zeros(lag_in.shape, BF16)

    prim_copy.wait()
    mine = gath.at[zh, x]
    mine[:, pl.ds(0, width)] = prim_in[0]
    mine[:, pl.ds(width, width)] = prim_in[1]

    az_rows = tap_rows(az_frac[0, 0], 256)
    rg_rows = tap_rows(rg_frac[0, 0], 256)
    span = rows_n + 2 * RIM
    az_taps = band(az_rows[:, :span], iota((rows_n, span), 1) - iota((rows_n, span), 0) - (az_off[0, 0] + RIM))
    rg_shape = (BLOCK + 2 * SIDE, BLOCK)
    rg_taps = band(rg_rows, iota(rg_shape, 0) - iota(rg_shape, 1) - (rg_off[0, 0] + SIDE))
    azim[:, pl.ds(0, SIDE)] = jnp.zeros((2 * rows_n, SIDE), BF16)
    azim[:, pl.ds(SIDE + cols_n, SIDE)] = jnp.zeros((2 * rows_n, SIDE), BF16)
    lanes = iota((1, mask.shape[1]), 1)
    marks = jnp.where(mask[...] != 0, 1.0, 0.0).astype(F32)
    picked = iota((LAG, mask.shape[1]), 1) == iota((LAG, mask.shape[1]), 0) + (rows_n - LAG)
    weight = jnp.sum(jnp.where(picked, marks, 0.0), axis=1, keepdims=True)
    count = jnp.sum(marks, axis=1, keepdims=True) * float(cols_n)

    pl.semaphore_wait(barrier, partners)

    z_copies = [
        remote(mine, mine, z_send.at[0], z_recv.at[0], t, date_at(z_at(1), x)),
        remote(mine, mine, z_send.at[1], z_recv.at[1], t, date_at(z_at(-1), x)),
    ]
    z_copies[0].start()
    z_copies[1].start()

    def spread(group, z):
        block = gath.at[z, x]
        copies = [
            remote(block, block, x_send.at[group, k - 1], x_recv.at[group, k - 1], t, date_at(zh, lax.rem(x + k, NX)))
            for k in (2, 1, 3)
        ]
        for copy in copies:
            copy.start()
        return copies

    x_copies = {0: spread(0, zh)}

    up = remote(sec.at[0, :, pl.ds(rows_n - RIM, RIM), :], ext.at[:, pl.ds(0, RIM), :], halo_send.at[0], halo_recv.at[0], lax.rem(t + 1, tiles), d)
    down = remote(sec.at[0, :, pl.ds(0, RIM), :], ext.at[:, pl.ds(RIM + rows_n, RIM), :], halo_send.at[1], halo_recv.at[1], lax.rem(t + tiles - 1, tiles), d)

    @pl.when(t < tiles - 1)
    def _():
        up.start()

    @pl.when(t > 0)
    def _():
        down.start()

    own_copy.wait()

    @pl.when(t > 0)
    def _():
        up.wait_recv()

    @pl.when(t < tiles - 1)
    def _():
        down.wait_recv()

    for plane in range(2):
        for b in range(cols_n // BLOCK):
            part = jnp.dot(az_taps, ext[plane, :, pl.ds(b * BLOCK, BLOCK)], preferred_element_type=F32)
            azim[pl.ds(plane * rows_n, rows_n), pl.ds(SIDE + b * BLOCK, BLOCK)] = part.astype(BF16)

    near = gath.at[z_at(-1), x]
    z_copies[0].wait_recv()
    relay = remote(near, near, z_send.at[2], z_recv.at[2], t, date_at(z_at(1), x))
    relay.start()
    x_copies[1] = spread(1, z_at(-1))
    z_copies[1].wait_recv()
    x_copies[2] = spread(2, z_at(1))

    for b in range(cols_n // BLOCK):
        part = jnp.dot(azim[:, pl.ds(b * BLOCK, BLOCK + 2 * SIDE)], rg_taps, preferred_element_type=F32).astype(BF16)
        for h in range(BLOCK // 128):
            half = part[:, h * 128 : (h + 1) * 128]
            res[b * (BLOCK // 128) + h] = half

    low_half = iota((rows_n, 128), 1) < width

    def beat(group, z):
        for copy in x_copies[group]:
            copy.wait_recv()
        for q in range(NX // 2):
            m = z * (NX // 2) + q
            a = gath[z, 2 * q].astype(F32)
            b = gath[z, 2 * q + 1].astype(F32)
            p_re = jnp.where(low_half, a, pltpu.roll(b, width, 1))
            p_im = jnp.where(low_half, pltpu.roll(a, width, 1), b)
            r_re = res[m, pl.ds(0, rows_n)].astype(F32)
            r_im = res[m, pl.ds(rows_n, rows_n)].astype(F32)
            i_re = p_re * r_re + p_im * r_im
            i_im = p_im * r_re - p_re * r_im
            ifg[m, pl.ds(0, rows_n)] = i_re
            ifg[m, pl.ds(rows_n, rows_n)] = i_im
            lag_out[z, q, 0] = i_re[:LAG].astype(BF16)
            lag_out[z, q, 1] = i_im[:LAG].astype(BF16)

    def lag_copy(z):
        return remote(lag_out.at[z], lag_in.at[z], lag_send.at[z], lag_recv.at[z], lax.rem(t + tiles - 1, tiles), d)

    def send_lag(z):
        @pl.when(t > 0)
        def _():
            lag_copy(z).start()

    zeros = jnp.zeros((8, 128), F32)

    def fold(v):
        return jnp.sum(v.reshape(LAG // 8, 8, 128), axis=0)

    def margin(z, sums):
        @pl.when(t < tiles - 1)
        def _():
            lag_copy(z).wait_recv()

        e_re, e_im, power = sums
        for q in range(NX // 2):
            m = z * (NX // 2) + q
            a_re = ifg[m, pl.ds(rows_n - LAG, LAG)]
            a_im = ifg[m, pl.ds(2 * rows_n - LAG, LAG)]
            l_re = lag_in[z, q, 0].astype(F32)
            l_im = lag_in[z, q, 1].astype(F32)
            e_re += fold(weight * (a_re * l_re + a_im * l_im))
            e_im += fold(weight * (a_im * l_re - a_re * l_im))
            power += fold((0.5 * weight) * (a_re * a_re + a_im * a_im + l_re * l_re + l_im * l_im))
        return e_re, e_im, power

    sums = (zeros, zeros, zeros)
    beat(0, zh)
    send_lag(zh)
    beat(1, z_at(-1))
    send_lag(z_at(-1))
    sums = margin(zh, sums)
    beat(2, z_at(1))
    send_lag(z_at(1))
    sums = margin(z_at(-1), sums)
    relay.wait_recv()
    x_copies[3] = spread(3, z_at(2))
    sums = margin(z_at(1), sums)
    beat(3, z_at(2))
    send_lag(z_at(2))
    sums = margin(z_at(2), sums)

    lane = iota((1, 128), 1)
    own = jnp.where(lane == 3, count, 0.0)
    for k, v in enumerate(sums):
        own = jnp.where(lane == k, jnp.sum(jnp.sum(v, axis=0, keepdims=True), axis=1, keepdims=True), own)
    stat_out[0] = own

    def stat_copy(k):
        return remote(stat_out, stat_in.at[pl.ds(tiles - 1 - k, 1)], stat_send, stat_recv, lax.rem(t + k, tiles), d)

    for k in range(1, tiles):
        stat_copy(k).start()

    total = jnp.zeros((2 * rows_n, 128), F32)
    per = 128 // LR
    for m in range(chunks):
        pick = jnp.where(iota((128, 128), 1) == m * per + iota((128, 128), 0) // LR, 1.0 / (LA * LR), 0.0).astype(BF16)
        v = ifg[m]
        hi = v.astype(BF16)
        lo = (v - hi.astype(F32)).astype(BF16)
        total += jnp.dot(hi, pick, preferred_element_type=F32) + jnp.dot(lo, pick, preferred_element_type=F32)
    acc[...] = total
    pairs = [acc[pl.ds(first, rows_n, stride=LA), :] for first in range(LA)]
    both = functools.reduce(lambda a, b: a + b, pairs)
    looks_re, looks_im = both[: rows_n // LA], both[rows_n // LA :]

    pltpu.make_async_copy(stat_in, stat_in, stat_recv).wait()
    grand = own + jnp.sum(stat_in[...], axis=0)
    t_re, t_im, t_pow, t_cnt = (jnp.sum(jnp.where(lane == k, grand, 0.0), axis=1, keepdims=True) for k in range(4))
    magnitude = jnp.sqrt(t_re * t_re + t_im * t_im)
    floor_val = (t_pow + 1e-06) / jnp.sqrt(jnp.maximum(t_cnt, 1.0))
    denom = jnp.maximum(magnitude, floor_val)
    u_re = t_re / denom
    u_im = t_im / denom
    out[0, 0] = looks_re * u_re + looks_im * u_im
    out[0, 1] = looks_im * u_re - looks_re * u_im

    for copy in z_copies:
        copy.wait_send()
    relay.wait_send()
    for group in range(4):
        for copy in x_copies[group]:
            copy.wait_send()

    @pl.when(t < tiles - 1)
    def _():
        up.wait_send()

    @pl.when(t > 0)
    def _():
        down.wait_send()
        for z in range(nz):
            lag_copy(z).wait_send()

    pltpu.make_async_copy(stat_in, stat_in, stat_send).wait()


def solution(mesh):
    tiles, dates = mesh.shape["tile"], mesh.shape["date"]
    nz = dates // NX

    def shards(secondary, primary, margin_mask, az_off, rg_off, az_frac, rg_frac):
        rows_n, cols_n = secondary.shape[2:]
        width = primary.shape[2]
        any_ = pl.BlockSpec(memory_space=pl.ANY)
        vmem = pl.BlockSpec(memory_space=pltpu.VMEM)
        smem = pl.BlockSpec(memory_space=pltpu.SMEM)
        dma = pltpu.SemaphoreType.DMA
        chunks = cols_n // 128
        return pl.pallas_call(
            functools.partial(kernel, tiles, dates),
            out_shape=jax.ShapeDtypeStruct((1, 2, rows_n // LA, cols_n // LR), F32),
            in_specs=[any_, any_, vmem, smem, smem, smem, smem],
            out_specs=vmem,
            scratch_shapes=[
                pltpu.VMEM((2, rows_n + 2 * RIM, cols_n), BF16),
                pltpu.VMEM((2, rows_n, width), BF16),
                pltpu.VMEM((2 * rows_n, cols_n + 2 * SIDE), BF16),
                pltpu.VMEM((nz, NX, rows_n, 2 * width), BF16),
                pltpu.VMEM((chunks, 2 * rows_n, 128), BF16),
                pltpu.VMEM((chunks, 2 * rows_n, 128), F32),
                pltpu.VMEM((nz, NX // 2, 2, LAG, 128), BF16),
                pltpu.VMEM((nz, NX // 2, 2, LAG, 128), BF16),
                pltpu.VMEM((1, 1, 128), F32),
                pltpu.VMEM((tiles - 1, 1, 128), F32),
                pltpu.VMEM((2 * rows_n, 128), F32),
                dma((2,)), dma((2,)), dma((2,)), dma((3,)), dma((3,)),
                dma((4, NX - 1)), dma((4, NX - 1)), dma((nz,)), dma((nz,)), dma, dma,
            ],
            compiler_params=pltpu.CompilerParams(collective_id=0, has_side_effects=True),
            name="coregister",
        )(secondary, primary, margin_mask.reshape(1, rows_n), az_off, rg_off, az_frac, rg_frac)

    return jax.shard_map(
        shards,
        mesh=mesh,
        in_specs=(
            P("date", None, "tile", None),
            P(None, "tile", "date"),
            P("tile"),
            P("date", "tile"),
            P("date", "tile"),
            P("date", "tile"),
            P("date", "tile"),
        ),
        out_specs=P("date", None, "tile", None),
        check_vma=False,
    )
```

```python
import functools

import jax
import jax.numpy as jnp
from jax import lax
from jax.experimental import pallas as pl
from jax.experimental.pallas import tpu as pltpu
from jax.sharding import PartitionSpec as P

LAG = 64
LA = 2
LR = 8
NX = 4
RIM = 32
SIDE = 128
BLOCK = 256
MESH = pl.DeviceIdType.MESH
F32 = jnp.float32
BF16 = jnp.bfloat16


def iota(shape, dim):
    return lax.broadcasted_iota(jnp.int32, shape, dim)


def tap_rows(frac, lanes):
    dist = iota((8, lanes), 0).astype(F32) - 3.0 - frac
    arg = jnp.pi * dist
    sinc = jnp.where(dist == 0.0, 1.0, jnp.sin(arg) / jnp.where(dist == 0.0, 1.0, arg))
    return sinc * (0.5 + 0.5 * jnp.cos(arg * 0.25))


def band(rows, first):
    total = jnp.zeros(first.shape, F32)
    for j in range(8):
        total = jnp.where(first == j - 3, rows[j : j + 1], total)
    return total.astype(BF16)


def kernel(
    tiles, dates,
    sec, prim, mask_at, az_off_at, rg_off_at, az_frac_at, rg_frac_at,
    out,
    mask, az_off, rg_off, az_frac, rg_frac,
    ext, prim_in, azim, gath, res, ifg, lag_out, lag_in, stat_out, stat_in, acc,
    local_sem, halo_send, halo_recv, z_send, z_recv, x_send, x_recv,
    lag_send, lag_recv, stat_send, stat_recv,
):
    nz = dates // NX
    rows_n = sec.shape[2]
    cols_n = sec.shape[3]
    width = prim.shape[0] // 2
    chunks = cols_n // 128
    t = lax.axis_index("tile")
    d = lax.axis_index("date")
    zh, x = d // NX, lax.rem(d, NX)
    step = 1 - 2 * lax.rem(t, 2)

    def z_at(k):
        return lax.rem(zh + k * step + 2 * nz, nz)

    def date_at(z, xx):
        return z * NX + xx

    def remote(src, dst, ss, rs, tile, date):
        return pltpu.make_async_remote_copy(
            src_ref=src, dst_ref=dst, send_sem=ss, recv_sem=rs,
            device_id={"tile": tile, "date": date}, device_id_type=MESH,
        )

    barrier = pltpu.get_barrier_semaphore()
    partners = 0
    for k in range(1, NX):
        pl.semaphore_signal(barrier, inc=1, device_id={"tile": t, "date": date_at(zh, lax.rem(x + k, NX))}, device_id_type=MESH)
        partners += 1
    for k in (1, -1):
        pl.semaphore_signal(barrier, inc=1, device_id={"tile": t, "date": date_at(z_at(k), x)}, device_id_type=MESH)
        partners += 1
    for k in range(1, tiles):
        pl.semaphore_signal(barrier, inc=1, device_id={"tile": lax.rem(t + k, tiles), "date": d}, device_id_type=MESH)
        partners += 1

    prim_copy = pltpu.make_async_copy(prim, prim_in, local_sem.at[0])
    prim_copy.start()
    small_copies = [
        pltpu.make_async_copy(src, dst, local_sem.at[2 + k])
        for k, (src, dst) in enumerate((
            (az_off_at, az_off), (rg_off_at, rg_off), (az_frac_at, az_frac), (rg_frac_at, rg_frac), (mask_at, mask),
        ))
    ]
    for copy in small_copies:
        copy.start()
    own_copy = pltpu.make_async_copy(sec.at[0], ext.at[:, pl.ds(RIM, rows_n), :], local_sem.at[1])
    own_copy.start()

    @pl.when(t == 0)
    def _():
        ext[:, pl.ds(0, RIM), :] = jnp.zeros((2, RIM, cols_n), BF16)

    @pl.when(t == tiles - 1)
    def _():
        ext[:, pl.ds(RIM + rows_n, RIM), :] = jnp.zeros((2, RIM, cols_n), BF16)
        lag_in[...] = jnp.zeros(lag_in.shape, BF16)

    prim_copy.wait()
    mine = gath.at[zh, x]
    mine[...] = prim_in[...].astype(F32).T.astype(BF16)

    pl.semaphore_wait(barrier, partners)

    z_copies = [
        remote(mine, mine, z_send.at[0], z_recv.at[0], t, date_at(z_at(1), x)),
        remote(mine, mine, z_send.at[1], z_recv.at[1], t, date_at(z_at(-1), x)),
    ]
    z_copies[0].start()
    z_copies[1].start()

    def spread(group, z):
        block = gath.at[z, x]
        copies = [
            remote(block, block, x_send.at[group, k - 1], x_recv.at[group, k - 1], t, date_at(zh, lax.rem(x + k, NX)))
            for k in (2, 1, 3)
        ]
        for copy in copies:
            copy.start()
        return copies

    x_copies = {0: spread(0, zh)}

    up = remote(sec.at[0, :, pl.ds(rows_n - RIM, RIM), :], ext.at[:, pl.ds(0, RIM), :], halo_send.at[0], halo_recv.at[0], lax.rem(t + 1, tiles), d)
    down = remote(sec.at[0, :, pl.ds(0, RIM), :], ext.at[:, pl.ds(RIM + rows_n, RIM), :], halo_send.at[1], halo_recv.at[1], lax.rem(t + tiles - 1, tiles), d)

    @pl.when(t < tiles - 1)
    def _():
        up.start()

    @pl.when(t > 0)
    def _():
        down.start()

    for copy in small_copies:
        copy.wait()
    az_rows = tap_rows(az_frac[...], 256)
    rg_rows = tap_rows(rg_frac[...], 256)
    span = rows_n + 2 * RIM
    az_taps = band(az_rows[:, :span], iota((rows_n, span), 1) - iota((rows_n, span), 0) - (az_off[...] + RIM))
    rg_shape = (BLOCK + 2 * SIDE, BLOCK)
    rg_taps = band(rg_rows, iota(rg_shape, 0) - iota(rg_shape, 1) - (rg_off[...] + SIDE))
    azim[:, pl.ds(0, SIDE)] = jnp.zeros((2 * rows_n, SIDE), BF16)
    azim[:, pl.ds(SIDE + cols_n, SIDE)] = jnp.zeros((2 * rows_n, SIDE), BF16)
    lanes = iota((1, mask.shape[1]), 1)
    marks = jnp.where(mask[...] != 0, 1.0, 0.0).astype(F32)
    picked = iota((LAG, mask.shape[1]), 1) == iota((LAG, mask.shape[1]), 0) + (rows_n - LAG)
    weight = jnp.sum(jnp.where(picked, marks, 0.0), axis=1, keepdims=True)
    count = jnp.sum(marks, axis=1, keepdims=True) * float(cols_n)

    own_copy.wait()

    @pl.when(t > 0)
    def _():
        up.wait_recv()

    @pl.when(t < tiles - 1)
    def _():
        down.wait_recv()

    for plane in range(2):
        for b in range(cols_n // BLOCK):
            part = jnp.dot(az_taps, ext[plane, :, pl.ds(b * BLOCK, BLOCK)], preferred_element_type=F32)
            azim[pl.ds(plane * rows_n, rows_n), pl.ds(SIDE + b * BLOCK, BLOCK)] = part.astype(BF16)

    near = gath.at[z_at(-1), x]
    z_copies[0].wait_recv()
    relay = remote(near, near, z_send.at[2], z_recv.at[2], t, date_at(z_at(1), x))
    relay.start()
    x_copies[1] = spread(1, z_at(-1))
    z_copies[1].wait_recv()
    x_copies[2] = spread(2, z_at(1))

    for b in range(cols_n // BLOCK):
        part = jnp.dot(azim[:, pl.ds(b * BLOCK, BLOCK + 2 * SIDE)], rg_taps, preferred_element_type=F32).astype(BF16)
        for h in range(BLOCK // 128):
            half = part[:, h * 128 : (h + 1) * 128]
            res[b * (BLOCK // 128) + h] = half

    low_half = iota((rows_n, 128), 1) < width

    def beat(group, z):
        for copy in x_copies[group]:
            copy.wait_recv()
        for q in range(NX // 2):
            m = z * (NX // 2) + q
            a = gath[z, 2 * q].astype(F32)
            b = gath[z, 2 * q + 1].astype(F32)
            p_re = jnp.where(low_half, a, pltpu.roll(b, width, 1))
            p_im = jnp.where(low_half, pltpu.roll(a, width, 1), b)
            r_re = res[m, pl.ds(0, rows_n)].astype(F32)
            r_im = res[m, pl.ds(rows_n, rows_n)].astype(F32)
            i_re = p_re * r_re + p_im * r_im
            i_im = p_im * r_re - p_re * r_im
            ifg[m, pl.ds(0, rows_n)] = i_re
            ifg[m, pl.ds(rows_n, rows_n)] = i_im
            lag_out[z, q, 0] = i_re[:LAG].astype(BF16)
            lag_out[z, q, 1] = i_im[:LAG].astype(BF16)

    def lag_copy(z):
        return remote(lag_out.at[z], lag_in.at[z], lag_send.at[z], lag_recv.at[z], lax.rem(t + tiles - 1, tiles), d)

    def send_lag(z):
        @pl.when(t > 0)
        def _():
            lag_copy(z).start()

    zeros = jnp.zeros((8, 128), F32)

    def fold(v):
        return jnp.sum(v.reshape(LAG // 8, 8, 128), axis=0)

    def margin(z, sums):
        @pl.when(t < tiles - 1)
        def _():
            lag_copy(z).wait_recv()

        e_re, e_im, power = sums
        for q in range(NX // 2):
            m = z * (NX // 2) + q
            a_re = ifg[m, pl.ds(rows_n - LAG, LAG)]
            a_im = ifg[m, pl.ds(2 * rows_n - LAG, LAG)]
            l_re = lag_in[z, q, 0].astype(F32)
            l_im = lag_in[z, q, 1].astype(F32)
            e_re += fold(weight * (a_re * l_re + a_im * l_im))
            e_im += fold(weight * (a_im * l_re - a_re * l_im))
            power += fold((0.5 * weight) * (a_re * a_re + a_im * a_im + l_re * l_re + l_im * l_im))
        return e_re, e_im, power

    sums = (zeros, zeros, zeros)
    beat(0, zh)
    send_lag(zh)
    beat(1, z_at(-1))
    send_lag(z_at(-1))
    sums = margin(zh, sums)
    beat(2, z_at(1))
    send_lag(z_at(1))
    sums = margin(z_at(-1), sums)
    relay.wait_recv()
    x_copies[3] = spread(3, z_at(2))
    sums = margin(z_at(1), sums)
    beat(3, z_at(2))
    send_lag(z_at(2))
    sums = margin(z_at(2), sums)

    lane = iota((1, 128), 1)
    own = jnp.where(lane == 3, count, 0.0)
    for k, v in enumerate(sums):
        own = jnp.where(lane == k, jnp.sum(jnp.sum(v, axis=0, keepdims=True), axis=1, keepdims=True), own)
    stat_out[0] = own

    def stat_copy(k):
        return remote(stat_out, stat_in.at[pl.ds(tiles - 1 - k, 1)], stat_send, stat_recv, lax.rem(t + k, tiles), d)

    for k in range(1, tiles):
        stat_copy(k).start()

    total = jnp.zeros((2 * rows_n, 128), F32)
    per = 128 // LR
    for m in range(chunks):
        pick = jnp.where(iota((128, 128), 1) == m * per + iota((128, 128), 0) // LR, 1.0 / (LA * LR), 0.0).astype(BF16)
        v = ifg[m]
        hi = v.astype(BF16)
        lo = (v - hi.astype(F32)).astype(BF16)
        total += jnp.dot(hi, pick, preferred_element_type=F32) + jnp.dot(lo, pick, preferred_element_type=F32)
    acc[...] = total
    pairs = [acc[pl.ds(first, rows_n, stride=LA), :] for first in range(LA)]
    both = functools.reduce(lambda a, b: a + b, pairs)
    looks_re, looks_im = both[: rows_n // LA], both[rows_n // LA :]

    pltpu.make_async_copy(stat_in, stat_in, stat_recv).wait()
    grand = own + jnp.sum(stat_in[...], axis=0)
    t_re, t_im, t_pow, t_cnt = (jnp.sum(jnp.where(lane == k, grand, 0.0), axis=1, keepdims=True) for k in range(4))
    magnitude = jnp.sqrt(t_re * t_re + t_im * t_im)
    floor_val = (t_pow + 1e-06) / jnp.sqrt(jnp.maximum(t_cnt, 1.0))
    denom = jnp.maximum(magnitude, floor_val)
    u_re = t_re / denom
    u_im = t_im / denom
    out[0, 0] = looks_re * u_re + looks_im * u_im
    out[0, 1] = looks_im * u_re - looks_re * u_im

    for copy in z_copies:
        copy.wait_send()
    relay.wait_send()
    for group in range(4):
        for copy in x_copies[group]:
            copy.wait_send()

    @pl.when(t < tiles - 1)
    def _():
        up.wait_send()

    @pl.when(t > 0)
    def _():
        down.wait_send()
        for z in range(nz):
            lag_copy(z).wait_send()

    pltpu.make_async_copy(stat_in, stat_in, stat_send).wait()


def solution(mesh):
    tiles, dates = mesh.shape["tile"], mesh.shape["date"]
    nz = dates // NX

    def shards(secondary, primary, margin_mask, az_off, rg_off, az_frac, rg_frac):
        rows_n, cols_n = secondary.shape[2:]
        width = primary.shape[2]
        any_ = pl.BlockSpec(memory_space=pl.ANY)
        vmem = pl.BlockSpec(memory_space=pltpu.VMEM)
        dma = pltpu.SemaphoreType.DMA
        chunks = cols_n // 128
        return pl.pallas_call(
            functools.partial(kernel, tiles, dates),
            out_shape=pltpu.VMEM((1, 2, rows_n // LA, cols_n // LR), F32),
            in_specs=[any_] * 7,
            out_specs=vmem,
            scratch_shapes=[
                pltpu.VMEM((1, rows_n), jnp.int32),
                *[pltpu.VMEM((1, 1), jnp.int32)] * 2,
                *[pltpu.VMEM((1, 1), F32)] * 2,
                pltpu.VMEM((2, rows_n + 2 * RIM, cols_n), BF16),
                pltpu.VMEM((2 * width, rows_n), BF16),
                pltpu.VMEM((2 * rows_n, cols_n + 2 * SIDE), BF16),
                pltpu.VMEM((nz, NX, rows_n, 2 * width), BF16),
                pltpu.VMEM((chunks, 2 * rows_n, 128), BF16),
                pltpu.VMEM((chunks, 2 * rows_n, 128), F32),
                pltpu.VMEM((nz, NX // 2, 2, LAG, 128), BF16),
                pltpu.VMEM((nz, NX // 2, 2, LAG, 128), BF16),
                pltpu.VMEM((1, 1, 128), F32),
                pltpu.VMEM((tiles - 1, 1, 128), F32),
                pltpu.VMEM((2 * rows_n, 128), F32),
                dma((7,)), dma((2,)), dma((2,)), dma((3,)), dma((3,)),
                dma((4, NX - 1)), dma((4, NX - 1)), dma((nz,)), dma((nz,)), dma, dma,
            ],
            compiler_params=pltpu.CompilerParams(collective_id=0, has_side_effects=True),
            name="coregister",
        )(secondary, primary.transpose(0, 2, 1).reshape(2 * width, rows_n), margin_mask.reshape(1, rows_n), az_off, rg_off, az_frac, rg_frac)

    return jax.shard_map(
        shards,
        mesh=mesh,
        in_specs=(
            P("date", None, "tile", None),
            P(None, "tile", "date"),
            P("tile"),
            P("date", "tile"),
            P("date", "tile"),
            P("date", "tile"),
            P("date", "tile"),
        ),
        out_specs=P("date", None, "tile", None),
        check_vma=False,
    )
```

```python
import functools

import jax
import jax.numpy as jnp
from jax import lax
from jax.experimental import pallas as pl
from jax.experimental.pallas import tpu as pltpu
from jax.sharding import PartitionSpec as P

LAG = 64
LA = 2
LR = 8
NX = 4
RIM = 32
SIDE = 128
BLOCK = 256
MESH = pl.DeviceIdType.MESH
ROUNDS = (1, 2, 4, 8, 16)
F32 = jnp.float32
BF16 = jnp.bfloat16


def iota(shape, dim):
    return lax.broadcasted_iota(jnp.int32, shape, dim)


def tap_rows(frac, lanes):
    dist = iota((8, lanes), 0).astype(F32) - 3.0 - frac
    arg = jnp.pi * dist
    sinc = jnp.where(dist == 0.0, 1.0, jnp.sin(arg) / jnp.where(dist == 0.0, 1.0, arg))
    return sinc * (0.5 + 0.5 * jnp.cos(arg * 0.25))


def band(rows, first):
    total = jnp.zeros(first.shape, F32)
    for j in range(8):
        total = jnp.where(first == j - 3, rows[j : j + 1], total)
    return total.astype(BF16)


def kernel(
    tiles, dates,
    sec, prim, mask_at, az_off_at, rg_off_at, az_frac_at, rg_frac_at,
    out,
    mask, az_off, rg_off, az_frac, rg_frac,
    ext, prim_in, azim, gath, res, ifg, lag_out, lag_in, stat_out, stat_in, acc,
    local_sem, halo_send, halo_recv, z_send, z_recv, x_send, x_recv,
    lag_send, lag_recv, stat_send, stat_recv,
    z_ready, x_ready, tile_ready, round_ready,
):
    nz = dates // NX
    rows_n = sec.shape[2]
    cols_n = sec.shape[3]
    width = prim.shape[0] // 2
    chunks = cols_n // 128
    t = lax.axis_index("tile")
    d = lax.axis_index("date")
    zh, x = d // NX, lax.rem(d, NX)

    def z_at(k):
        return lax.rem(zh + k + nz, nz)

    def date_at(z, xx):
        return z * NX + xx

    def remote(src, dst, ss, rs, tile, date):
        return pltpu.make_async_remote_copy(
            src_ref=src, dst_ref=dst, send_sem=ss, recv_sem=rs,
            device_id={"tile": tile, "date": date}, device_id_type=MESH,
        )

    def order(z):
        return jnp.where(z >= 2, 5 - z, z)

    def x_at(k):
        return lax.rem(x + k, NX)

    def signal(sem, tile, date):
        pl.semaphore_signal(sem, inc=1, device_id={"tile": tile, "date": date}, device_id_type=MESH)

    z_first = {k: order(zh) < order(z_at(k)) for k in range(1, nz)}
    x_first = {k: x < x_at(k) for k in range(1, NX)}
    barrier = pltpu.get_barrier_semaphore()
    for k in range(1, nz):
        @pl.when(z_first[k])
        def _(k=k):
            signal(barrier, t, date_at(z_at(k), x))
    for k in range(1, NX):
        @pl.when(x_first[k])
        def _(k=k):
            signal(barrier, t, date_at(zh, x_at(k)))

    @pl.when(t < tiles - 1)
    def _():
        signal(barrier, t + 1, d)

    small_copies = [
        pltpu.make_async_copy(src, dst, local_sem.at[2 + k])
        for k, (src, dst) in enumerate((
            (az_off_at, az_off), (rg_off_at, rg_off), (az_frac_at, az_frac), (rg_frac_at, rg_frac), (mask_at, mask),
        ))
    ]
    for copy in small_copies:
        copy.start()
    prim_copy = pltpu.make_async_copy(prim, prim_in, local_sem.at[0])
    prim_copy.start()
    own_copy = pltpu.make_async_copy(sec.at[0], ext.at[:, pl.ds(RIM, rows_n), :], local_sem.at[1])
    own_copy.start()

    @pl.when(t == 0)
    def _():
        ext[:, pl.ds(0, RIM), :] = jnp.zeros((2, RIM, cols_n), BF16)

    @pl.when(t == tiles - 1)
    def _():
        ext[:, pl.ds(RIM + rows_n, RIM), :] = jnp.zeros((2, RIM, cols_n), BF16)
        lag_in[...] = jnp.zeros(lag_in.shape, BF16)

    prim_copy.wait()
    mine = gath.at[zh, x]
    mine[...] = prim_in[...].astype(F32).T.astype(BF16)

    before = order(zh) + x + jnp.where(t > 0, 1, 0)

    @pl.when(before > 0)
    def _():
        pl.semaphore_wait(barrier, before)

    for k in range(1, nz):
        @pl.when(jnp.logical_not(z_first[k]))
        def _(k=k):
            signal(z_ready.at[nz - k - 1], t, date_at(z_at(k), x))
    for k in range(1, NX):
        @pl.when(jnp.logical_not(x_first[k]))
        def _(k=k):
            signal(x_ready.at[NX - k - 1], t, date_at(zh, x_at(k)))

    @pl.when(t > 0)
    def _():
        signal(tile_ready, t - 1, d)

    z_copies = {
        k: remote(mine, mine, z_send.at[k - 1], z_recv.at[nz - k - 1], t, date_at(z_at(k), x))
        for k in range(1, nz)
    }

    def x_copy(group, z, k):
        block = gath.at[z, x]
        return remote(block, block, x_send.at[group, k - 1], x_recv.at[group, k - 1], t, date_at(zh, x_at(k)))

    for k in (2, 1, 3):
        @pl.when(jnp.logical_not(z_first[k]))
        def _(k=k):
            z_copies[k].start()
    for k in (2, 1, 3):
        @pl.when(jnp.logical_not(x_first[k]))
        def _(k=k):
            x_copy(0, zh, k).start()

    up = remote(sec.at[0, :, pl.ds(rows_n - RIM, RIM), :], ext.at[:, pl.ds(0, RIM), :], halo_send.at[0], halo_recv.at[0], lax.rem(t + 1, tiles), d)
    down = remote(sec.at[0, :, pl.ds(0, RIM), :], ext.at[:, pl.ds(RIM + rows_n, RIM), :], halo_send.at[1], halo_recv.at[1], lax.rem(t + tiles - 1, tiles), d)

    @pl.when(t > 0)
    def _():
        down.start()

    for k in (1, 2, 3):
        @pl.when(x_first[k])
        def _(k=k):
            pl.semaphore_wait(x_ready.at[k - 1], 1)
            x_copy(0, zh, k).start()

    @pl.when(t < tiles - 1)
    def _():
        pl.semaphore_wait(tile_ready, 1)
        up.start()

    def round_signal(i):
        @pl.when(t >= ROUNDS[i])
        def _():
            signal(round_ready.at[i], t - ROUNDS[i], d)

        @pl.when(t < tiles - ROUNDS[i])
        def _():
            signal(round_ready.at[i], t + ROUNDS[i], d)

    def round_wait(i):
        expected = jnp.where(t >= ROUNDS[i], 1, 0) + jnp.where(t < tiles - ROUNDS[i], 1, 0)

        @pl.when(expected > 0)
        def _():
            pl.semaphore_wait(round_ready.at[i], expected)

    def spread(group, z):
        for k in (2, 1, 3):
            x_copy(group, z, k).start()

    def turn(k):
        @pl.when(z_first[k])
        def _():
            pl.semaphore_wait(z_ready.at[k - 1], 1)
            z_copies[k].start()

    def arrive(k):
        block = gath.at[z_at(k), x]
        remote(block, block, z_send.at[k - 1], z_recv.at[k - 1], t, date_at(z_at(k), x)).wait_recv()
        spread(k, z_at(k))

    round_signal(0)

    for copy in small_copies:
        copy.wait()
    az_rows = tap_rows(az_frac[...], 256)
    rg_rows = tap_rows(rg_frac[...], 256)
    span = rows_n + 2 * RIM
    az_taps = band(az_rows[:, :span], iota((rows_n, span), 1) - iota((rows_n, span), 0) - (az_off[...] + RIM))
    rg_shape = (BLOCK + 2 * SIDE, BLOCK)
    rg_taps = band(rg_rows, iota(rg_shape, 0) - iota(rg_shape, 1) - (rg_off[...] + SIDE))
    azim[:, pl.ds(0, SIDE)] = jnp.zeros((2 * rows_n, SIDE), BF16)
    azim[:, pl.ds(SIDE + cols_n, SIDE)] = jnp.zeros((2 * rows_n, SIDE), BF16)
    lanes = iota((1, mask.shape[1]), 1)
    marks = jnp.where(mask[...] != 0, 1.0, 0.0).astype(F32)
    picked = iota((LAG, mask.shape[1]), 1) == iota((LAG, mask.shape[1]), 0) + (rows_n - LAG)
    weight = jnp.sum(jnp.where(picked, marks, 0.0), axis=1, keepdims=True)
    count = jnp.sum(marks, axis=1, keepdims=True) * float(cols_n)

    own_copy.wait()

    @pl.when(t > 0)
    def _():
        up.wait_recv()

    @pl.when(t < tiles - 1)
    def _():
        down.wait_recv()

    for plane in range(2):
        for b in range(cols_n // BLOCK):
            part = jnp.dot(az_taps, ext[plane, :, pl.ds(b * BLOCK, BLOCK)], preferred_element_type=F32)
            azim[pl.ds(plane * rows_n, rows_n), pl.ds(SIDE + b * BLOCK, BLOCK)] = part.astype(BF16)

    round_wait(0)
    round_signal(1)

    for b in range(cols_n // BLOCK):
        part = jnp.dot(azim[:, pl.ds(b * BLOCK, BLOCK + 2 * SIDE)], rg_taps, preferred_element_type=F32).astype(BF16)
        for h in range(BLOCK // 128):
            half = part[:, h * 128 : (h + 1) * 128]
            res[b * (BLOCK // 128) + h] = half

    round_wait(1)
    round_signal(2)
    turn(1)
    arrive(1)
    round_wait(2)
    round_signal(3)
    turn(3)
    arrive(3)
    round_wait(3)
    round_signal(4)
    turn(2)

    low_half = iota((rows_n, 128), 1) < width

    def beat(group, z):
        for k in range(1, NX):
            x_copy(group, z, k).wait_recv()
        for q in range(NX // 2):
            m = z * (NX // 2) + q
            a = gath[z, 2 * q].astype(F32)
            b = gath[z, 2 * q + 1].astype(F32)
            p_re = jnp.where(low_half, a, pltpu.roll(b, width, 1))
            p_im = jnp.where(low_half, pltpu.roll(a, width, 1), b)
            r_re = res[m, pl.ds(0, rows_n)].astype(F32)
            r_im = res[m, pl.ds(rows_n, rows_n)].astype(F32)
            i_re = p_re * r_re + p_im * r_im
            i_im = p_im * r_re - p_re * r_im
            ifg[m, pl.ds(0, rows_n)] = i_re
            ifg[m, pl.ds(rows_n, rows_n)] = i_im
            lag_out[z, q, 0] = i_re[:LAG].astype(BF16)
            lag_out[z, q, 1] = i_im[:LAG].astype(BF16)

    def lag_copy(z):
        return remote(lag_out.at[z], lag_in.at[z], lag_send.at[z], lag_recv.at[z], lax.rem(t + tiles - 1, tiles), d)

    def send_lag(z):
        @pl.when(t > 0)
        def _():
            lag_copy(z).start()

    zeros = jnp.zeros((8, 128), F32)

    def fold(v):
        return jnp.sum(v.reshape(LAG // 8, 8, 128), axis=0)

    def margin(z, sums):
        @pl.when(t < tiles - 1)
        def _():
            lag_copy(z).wait_recv()

        e_re, e_im, power = sums
        for q in range(NX // 2):
            m = z * (NX // 2) + q
            a_re = ifg[m, pl.ds(rows_n - LAG, LAG)]
            a_im = ifg[m, pl.ds(2 * rows_n - LAG, LAG)]
            l_re = lag_in[z, q, 0].astype(F32)
            l_im = lag_in[z, q, 1].astype(F32)
            e_re += fold(weight * (a_re * l_re + a_im * l_im))
            e_im += fold(weight * (a_im * l_re - a_re * l_im))
            power += fold((0.5 * weight) * (a_re * a_re + a_im * a_im + l_re * l_re + l_im * l_im))
        return e_re, e_im, power

    sums = (zeros, zeros, zeros)
    beat(0, zh)
    send_lag(zh)
    beat(1, z_at(1))
    send_lag(z_at(1))
    sums = margin(zh, sums)
    beat(3, z_at(3))
    send_lag(z_at(3))
    sums = margin(z_at(1), sums)
    arrive(2)
    sums = margin(z_at(3), sums)
    beat(2, z_at(2))
    send_lag(z_at(2))
    round_wait(4)
    sums = margin(z_at(2), sums)

    lane = iota((1, 128), 1)
    own = jnp.where(lane == 3, count, 0.0)
    for k, v in enumerate(sums):
        own = jnp.where(lane == k, jnp.sum(jnp.sum(v, axis=0, keepdims=True), axis=1, keepdims=True), own)
    stat_out[0] = own

    def stat_copy(k):
        return remote(stat_out, stat_in.at[pl.ds(tiles - 1 - k, 1)], stat_send, stat_recv, lax.rem(t + k, tiles), d)

    for k in range(1, tiles):
        stat_copy(k).start()

    total = jnp.zeros((2 * rows_n, 128), F32)
    per = 128 // LR
    for m in range(chunks):
        pick = jnp.where(iota((128, 128), 1) == m * per + iota((128, 128), 0) // LR, 1.0 / (LA * LR), 0.0).astype(BF16)
        v = ifg[m]
        hi = v.astype(BF16)
        lo = (v - hi.astype(F32)).astype(BF16)
        total += jnp.dot(hi, pick, preferred_element_type=F32) + jnp.dot(lo, pick, preferred_element_type=F32)
    acc[...] = total
    pairs = [acc[pl.ds(first, rows_n, stride=LA), :] for first in range(LA)]
    both = functools.reduce(lambda a, b: a + b, pairs)
    looks_re, looks_im = both[: rows_n // LA], both[rows_n // LA :]

    pltpu.make_async_copy(stat_in, stat_in, stat_recv).wait()
    grand = own + jnp.sum(stat_in[...], axis=0)
    t_re, t_im, t_pow, t_cnt = (jnp.sum(jnp.where(lane == k, grand, 0.0), axis=1, keepdims=True) for k in range(4))
    magnitude = jnp.sqrt(t_re * t_re + t_im * t_im)
    floor_val = (t_pow + 1e-06) / jnp.sqrt(jnp.maximum(t_cnt, 1.0))
    denom = jnp.maximum(magnitude, floor_val)
    u_re = t_re / denom
    u_im = t_im / denom
    out[0, 0] = looks_re * u_re + looks_im * u_im
    out[0, 1] = looks_im * u_re - looks_re * u_im

    for k in range(1, nz):
        z_copies[k].wait_send()
    for group in range(nz):
        for k in range(1, NX):
            x_copy(group, z_at(group), k).wait_send()

    @pl.when(t < tiles - 1)
    def _():
        up.wait_send()

    @pl.when(t > 0)
    def _():
        down.wait_send()
        for z in range(nz):
            lag_copy(z).wait_send()

    pltpu.make_async_copy(stat_in, stat_in, stat_send).wait()


def solution(mesh):
    tiles, dates = mesh.shape["tile"], mesh.shape["date"]
    nz = dates // NX

    def shards(secondary, primary, margin_mask, az_off, rg_off, az_frac, rg_frac):
        rows_n, cols_n = secondary.shape[2:]
        width = primary.shape[2]
        hbm = pl.BlockSpec(memory_space=pltpu.HBM)
        vmem = pl.BlockSpec(memory_space=pltpu.VMEM)
        dma = pltpu.SemaphoreType.DMA
        regular = pltpu.SemaphoreType.REGULAR
        chunks = cols_n // 128
        return pl.pallas_call(
            functools.partial(kernel, tiles, dates),
            out_shape=pltpu.VMEM((1, 2, rows_n // LA, cols_n // LR), F32),
            in_specs=[hbm] * 7,
            out_specs=vmem,
            scratch_shapes=[
                pltpu.VMEM((1, rows_n), jnp.int32),
                *[pltpu.VMEM((1, 1), jnp.int32)] * 2,
                *[pltpu.VMEM((1, 1), F32)] * 2,
                pltpu.VMEM((2, rows_n + 2 * RIM, cols_n), BF16),
                pltpu.VMEM((2 * width, rows_n), BF16),
                pltpu.VMEM((2 * rows_n, cols_n + 2 * SIDE), BF16),
                pltpu.VMEM((nz, NX, rows_n, 2 * width), BF16),
                pltpu.VMEM((chunks, 2 * rows_n, 128), BF16),
                pltpu.VMEM((chunks, 2 * rows_n, 128), F32),
                pltpu.VMEM((nz, NX // 2, 2, LAG, 128), BF16),
                pltpu.VMEM((nz, NX // 2, 2, LAG, 128), BF16),
                pltpu.VMEM((1, 1, 128), F32),
                pltpu.VMEM((tiles - 1, 1, 128), F32),
                pltpu.VMEM((2 * rows_n, 128), F32),
                dma((7,)), dma((2,)), dma((2,)), dma((3,)), dma((3,)),
                dma((4, NX - 1)), dma((4, NX - 1)), dma((nz,)), dma((nz,)), dma, dma,
                regular((nz - 1,)), regular((NX - 1,)), regular, regular((len(ROUNDS),)),
            ],
            compiler_params=pltpu.CompilerParams(collective_id=0, has_side_effects=True),
            name="coregister",
        )(secondary, primary.transpose(0, 2, 1).reshape(2 * width, rows_n), margin_mask.reshape(1, rows_n), az_off, rg_off, az_frac, rg_frac)

    return jax.shard_map(
        shards,
        mesh=mesh,
        in_specs=(
            P("date", None, "tile", None),
            P(None, "tile", "date"),
            P("tile"),
            P("date", "tile"),
            P("date", "tile"),
            P("date", "tile"),
            P("date", "tile"),
        ),
        out_specs=P("date", None, "tile", None),
        check_vma=False,
    )
```

```python
import functools

import jax
import jax.numpy as jnp
from jax import lax
from jax.experimental import pallas as pl
from jax.experimental.pallas import tpu as pltpu
from jax.sharding import PartitionSpec as P

LAG = 64
LA = 2
LR = 8
NX = 4
RIM = 32
SIDE = 128
BLOCK = 256
MESH = pl.DeviceIdType.MESH
ROUNDS = (1, 2, 4, 8, 16)
F32 = jnp.float32
BF16 = jnp.bfloat16


def iota(shape, dim):
    return lax.broadcasted_iota(jnp.int32, shape, dim)


def tap_rows(frac, lanes):
    dist = iota((8, lanes), 0).astype(F32) - 3.0 - frac
    arg = jnp.pi * dist
    sinc = jnp.where(dist == 0.0, 1.0, jnp.sin(arg) / jnp.where(dist == 0.0, 1.0, arg))
    return sinc * (0.5 + 0.5 * jnp.cos(arg * 0.25))


def band(rows, first):
    total = jnp.zeros(first.shape, F32)
    for j in range(8):
        total = jnp.where(first == j - 3, rows[j : j + 1], total)
    return total.astype(BF16)


def kernel(
    tiles, dates,
    sec, prim, mask_at, az_off_at, rg_off_at, az_frac_at, rg_frac_at,
    out,
    mask, az_off, rg_off, az_frac, rg_frac,
    ext, prim_in, azim, gath, res, ifg, gnext, rnext, stat_out, stat_in, acc,
    local_sem, halo_send, halo_recv, z_send, z_recv, x_send, x_recv,
    next_send, next_recv, row_send, row_recv, stat_send, stat_recv,
    z_ready, x_ready, tile_ready, round_ready,
):
    nz = dates // NX
    rows_n = sec.shape[2]
    cols_n = sec.shape[3]
    width = prim.shape[0] // 2
    chunks = cols_n // 128
    t = lax.axis_index("tile")
    d = lax.axis_index("date")
    zh, x = d // NX, lax.rem(d, NX)

    def z_at(k):
        return lax.rem(zh + k + nz, nz)

    def date_at(z, xx):
        return z * NX + xx

    def remote(src, dst, ss, rs, tile, date):
        return pltpu.make_async_remote_copy(
            src_ref=src, dst_ref=dst, send_sem=ss, recv_sem=rs,
            device_id={"tile": tile, "date": date}, device_id_type=MESH,
        )

    def order(z):
        return jnp.where(z >= 2, 5 - z, z)

    def x_at(k):
        return lax.rem(x + k, NX)

    def signal(sem, tile, date):
        pl.semaphore_signal(sem, inc=1, device_id={"tile": tile, "date": date}, device_id_type=MESH)

    z_first = {k: order(zh) < order(z_at(k)) for k in range(1, nz)}
    x_first = {k: x < x_at(k) for k in range(1, NX)}
    barrier = pltpu.get_barrier_semaphore()
    for k in range(1, nz):
        @pl.when(z_first[k])
        def _(k=k):
            signal(barrier, t, date_at(z_at(k), x))
    for k in range(1, NX):
        @pl.when(x_first[k])
        def _(k=k):
            signal(barrier, t, date_at(zh, x_at(k)))

    @pl.when(t < tiles - 1)
    def _():
        signal(barrier, t + 1, d)

    small_copies = [
        pltpu.make_async_copy(src, dst, local_sem.at[2 + k])
        for k, (src, dst) in enumerate((
            (az_off_at, az_off), (rg_off_at, rg_off), (az_frac_at, az_frac), (rg_frac_at, rg_frac), (mask_at, mask),
        ))
    ]
    for copy in small_copies:
        copy.start()
    prim_copy = pltpu.make_async_copy(prim, prim_in, local_sem.at[0])
    prim_copy.start()
    own_copy = pltpu.make_async_copy(sec.at[0], ext.at[:, pl.ds(RIM, rows_n), :], local_sem.at[1])
    own_copy.start()

    @pl.when(t == 0)
    def _():
        ext[:, pl.ds(0, RIM), :] = jnp.zeros((2, RIM, cols_n), BF16)

    @pl.when(t == tiles - 1)
    def _():
        ext[:, pl.ds(RIM + rows_n, RIM), :] = jnp.zeros((2, RIM, cols_n), BF16)
        gnext[...] = jnp.zeros(gnext.shape, BF16)
        rnext[...] = jnp.zeros(rnext.shape, BF16)

    prim_copy.wait()
    mine = gath.at[zh, x]
    mine[...] = prim_in[...].astype(F32).T.astype(BF16)

    before = order(zh) + x + jnp.where(t > 0, 1, 0)

    @pl.when(before > 0)
    def _():
        pl.semaphore_wait(barrier, before)

    for k in (1, nz - 1):
        @pl.when(jnp.logical_not(z_first[k]))
        def _(k=k):
            signal(z_ready.at[nz - k - 1], t, date_at(z_at(k), x))
    for k in range(1, NX):
        @pl.when(jnp.logical_not(x_first[k]))
        def _(k=k):
            signal(x_ready.at[NX - k - 1], t, date_at(zh, x_at(k)))

    @pl.when(t > 0)
    def _():
        signal(tile_ready, t - 1, d)

    z_copies = {
        k: remote(mine, mine, z_send.at[k - 1], z_recv.at[nz - k - 1], t, date_at(z_at(k), x))
        for k in range(1, nz)
    }

    def x_copy(group, z, k):
        block = gath.at[z, x]
        return remote(block, block, x_send.at[group, k - 1], x_recv.at[group, k - 1], t, date_at(zh, x_at(k)))

    for k in (2, 1, 3):
        @pl.when(jnp.logical_not(z_first[k]))
        def _(k=k):
            z_copies[k].start()
    for k in (2, 1, 3):
        @pl.when(jnp.logical_not(x_first[k]))
        def _(k=k):
            x_copy(0, zh, k).start()

    up = remote(sec.at[0, :, pl.ds(rows_n - RIM, RIM), :], ext.at[:, pl.ds(0, RIM), :], halo_send.at[0], halo_recv.at[0], lax.rem(t + 1, tiles), d)
    down = remote(sec.at[0, :, pl.ds(0, RIM), :], ext.at[:, pl.ds(RIM + rows_n, RIM), :], halo_send.at[1], halo_recv.at[1], lax.rem(t + tiles - 1, tiles), d)

    @pl.when(t > 0)
    def _():
        down.start()

    for k in range(1, NX):
        @pl.when(x_first[k])
        def _(k=k):
            pl.semaphore_wait(x_ready.at[k - 1], 1)
            x_copy(0, zh, k).start()
            signal(x_ready.at[NX - k - 1], t, date_at(zh, x_at(k)))

    @pl.when(t < tiles - 1)
    def _():
        pl.semaphore_wait(tile_ready, 1)
        up.start()

    def round_signal(i):
        @pl.when(t >= ROUNDS[i])
        def _():
            signal(round_ready.at[i], t - ROUNDS[i], d)

        @pl.when(t < tiles - ROUNDS[i])
        def _():
            signal(round_ready.at[i], t + ROUNDS[i], d)

    def round_wait(i):
        expected = jnp.where(t >= ROUNDS[i], 1, 0) + jnp.where(t < tiles - ROUNDS[i], 1, 0)

        @pl.when(expected > 0)
        def _():
            pl.semaphore_wait(round_ready.at[i], expected)

    def next_copy(group, z, k):
        return remote(
            gath.at[z, x, pl.ds(0, LAG), :], gnext.at[z, x], next_send.at[group, k], next_recv.at[group, k],
            lax.rem(t + tiles - 1, tiles), date_at(zh, x_at(k)),
        )

    def spread_back(group, z):
        @pl.when(t > 0)
        def _():
            for k in (2, 1, 3, 0):
                next_copy(group, z, k).start()

    def spread(group, z):
        spread_back(group, z)
        for k in (2, 1, 3):
            x_copy(group, z, k).start()

    def turn(k):
        @pl.when(z_first[k])
        def _():
            pl.semaphore_wait(z_ready.at[k - 1], 1)
            z_copies[k].start()

    def arrive(k):
        block = gath.at[z_at(k), x]
        remote(block, block, z_send.at[k - 1], z_recv.at[k - 1], t, date_at(z_at(k), x)).wait_recv()
        spread(k, z_at(k))

    def pass_on(of, to):
        block = gath.at[z_at(of), x]
        return remote(block, block, z_send.at[1], z_recv.at[1], t, date_at(z_at(to), x))

    for k in range(1, NX):
        @pl.when(jnp.logical_not(x_first[k]))
        def _(k=k):
            pl.semaphore_wait(x_ready.at[k - 1], 1)
    spread_back(0, zh)

    round_signal(0)

    for copy in small_copies:
        copy.wait()
    az_rows = tap_rows(az_frac[...], 256)
    rg_rows = tap_rows(rg_frac[...], 256)
    span = rows_n + 2 * RIM
    az_taps = band(az_rows[:, :span], iota((rows_n, span), 1) - iota((rows_n, span), 0) - (az_off[...] + RIM))
    rg_shape = (BLOCK + 2 * SIDE, BLOCK)
    rg_taps = band(rg_rows, iota(rg_shape, 0) - iota(rg_shape, 1) - (rg_off[...] + SIDE))
    azim[:, pl.ds(0, SIDE)] = jnp.zeros((2 * rows_n, SIDE), BF16)
    azim[:, pl.ds(SIDE + cols_n, SIDE)] = jnp.zeros((2 * rows_n, SIDE), BF16)
    lanes = iota((1, mask.shape[1]), 1)
    marks = jnp.where(mask[...] != 0, 1.0, 0.0).astype(F32)
    picked = iota((LAG, mask.shape[1]), 1) == iota((LAG, mask.shape[1]), 0) + (rows_n - LAG)
    weight = jnp.sum(jnp.where(picked, marks, 0.0), axis=1, keepdims=True)
    count = jnp.sum(marks, axis=1, keepdims=True) * float(cols_n)

    own_copy.wait()

    @pl.when(t > 0)
    def _():
        up.wait_recv()

    @pl.when(t < tiles - 1)
    def _():
        down.wait_recv()

    for plane in range(2):
        for b in range(cols_n // BLOCK):
            part = jnp.dot(az_taps, ext[plane, :, pl.ds(b * BLOCK, BLOCK)], preferred_element_type=F32)
            azim[pl.ds(plane * rows_n, rows_n), pl.ds(SIDE + b * BLOCK, BLOCK)] = part.astype(BF16)

    round_wait(0)
    round_signal(1)

    for b in range(cols_n // BLOCK):
        part = jnp.dot(azim[:, pl.ds(b * BLOCK, BLOCK + 2 * SIDE)], rg_taps, preferred_element_type=F32).astype(BF16)
        for h in range(BLOCK // 128):
            half = part[:, h * 128 : (h + 1) * 128]
            res[b * (BLOCK // 128) + h] = half

    def row_copy(plane):
        return remote(
            res.at[:, pl.ds(plane * rows_n, LAG), :], rnext.at[plane], row_send.at[plane], row_recv.at[plane],
            lax.rem(t + tiles - 1, tiles), d,
        )

    round_wait(1)
    round_signal(2)

    @pl.when(t > 0)
    def _():
        row_copy(0).start()
        row_copy(1).start()

    turn(1)
    arrive(1)
    round_wait(2)
    round_signal(3)
    turn(3)

    @pl.when(zh == 0)
    def _():
        pass_on(1, 3).start()

    arrive(3)

    @pl.when(zh == 1)
    def _():
        pass_on(3, 1).start()

    round_wait(3)
    round_signal(4)

    @pl.when(t < tiles - 1)
    def _():
        row_copy(0).wait_recv()
        row_copy(1).wait_recv()

    low_half = iota((rows_n, 128), 1) < width

    def product(block_of, z, q, r_re, r_im, low):
        a = block_of[z, 2 * q].astype(F32)
        b = block_of[z, 2 * q + 1].astype(F32)
        p_re = jnp.where(low, a, pltpu.roll(b, width, 1))
        p_im = jnp.where(low, pltpu.roll(a, width, 1), b)
        return p_re * r_re + p_im * r_im, p_im * r_re - p_re * r_im

    def fold(v):
        return jnp.sum(v.reshape(LAG // 8, 8, 128), axis=0)

    def beat(group, z, sums):
        for k in range(1, NX):
            x_copy(group, z, k).wait_recv()

        @pl.when(t < tiles - 1)
        def _():
            for k in range(NX):
                next_copy(group, z, k).wait_recv()

        e_re, e_im, power = sums
        for q in range(NX // 2):
            m = z * (NX // 2) + q
            i_re, i_im = product(
                gath, z, q, res[m, pl.ds(0, rows_n)].astype(F32), res[m, pl.ds(rows_n, rows_n)].astype(F32), low_half
            )
            ifg[m, pl.ds(0, rows_n)] = i_re
            ifg[m, pl.ds(rows_n, rows_n)] = i_im
            l_re, l_im = product(gnext, z, q, rnext[0, m].astype(F32), rnext[1, m].astype(F32), low_half[:LAG])
            a_re, a_im = i_re[rows_n - LAG :], i_im[rows_n - LAG :]
            e_re += fold(weight * (a_re * l_re + a_im * l_im))
            e_im += fold(weight * (a_im * l_re - a_re * l_im))
            power += fold((0.5 * weight) * (a_re * a_re + a_im * a_im + l_re * l_re + l_im * l_im))
        return e_re, e_im, power

    zeros = jnp.zeros((8, 128), F32)
    sums = beat(0, zh, (zeros, zeros, zeros))
    sums = beat(1, z_at(1), sums)
    sums = beat(3, z_at(3), sums)
    round_wait(4)
    arrive(2)
    sums = beat(2, z_at(2), sums)

    lane = iota((1, 128), 1)
    own = jnp.where(lane == 3, count, 0.0)
    for k, v in enumerate(sums):
        own = jnp.where(lane == k, jnp.sum(jnp.sum(v, axis=0, keepdims=True), axis=1, keepdims=True), own)
    stat_out[0] = own

    def stat_copy(k):
        return remote(stat_out, stat_in.at[pl.ds(tiles - 1 - k, 1)], stat_send, stat_recv, lax.rem(t + k, tiles), d)

    for k in range(1, tiles):
        stat_copy(k).start()

    total = jnp.zeros((2 * rows_n, 128), F32)
    per = 128 // LR
    for m in range(chunks):
        pick = jnp.where(iota((128, 128), 1) == m * per + iota((128, 128), 0) // LR, 1.0 / (LA * LR), 0.0).astype(BF16)
        v = ifg[m]
        hi = v.astype(BF16)
        lo = (v - hi.astype(F32)).astype(BF16)
        total += jnp.dot(hi, pick, preferred_element_type=F32) + jnp.dot(lo, pick, preferred_element_type=F32)
    acc[...] = total
    pairs = [acc[pl.ds(first, rows_n, stride=LA), :] for first in range(LA)]
    both = functools.reduce(lambda a, b: a + b, pairs)
    looks_re, looks_im = both[: rows_n // LA], both[rows_n // LA :]

    pltpu.make_async_copy(stat_in, stat_in, stat_recv).wait()
    grand = own + jnp.sum(stat_in[...], axis=0)
    t_re, t_im, t_pow, t_cnt = (jnp.sum(jnp.where(lane == k, grand, 0.0), axis=1, keepdims=True) for k in range(4))
    magnitude = jnp.sqrt(t_re * t_re + t_im * t_im)
    floor_val = (t_pow + 1e-06) / jnp.sqrt(jnp.maximum(t_cnt, 1.0))
    denom = jnp.maximum(magnitude, floor_val)
    u_re = t_re / denom
    u_im = t_im / denom
    out[0, 0] = looks_re * u_re + looks_im * u_im
    out[0, 1] = looks_im * u_re - looks_re * u_im

    for k in range(1, nz):
        z_copies[k].wait_send()
    for group in range(nz):
        for k in range(1, NX):
            x_copy(group, z_at(group), k).wait_send()

    @pl.when(t < tiles - 1)
    def _():
        up.wait_send()

    @pl.when(t > 0)
    def _():
        down.wait_send()
        for group in range(nz):
            for k in range(NX):
                next_copy(group, z_at(group), k).wait_send()
        row_copy(0).wait_send()
        row_copy(1).wait_send()

    pltpu.make_async_copy(stat_in, stat_in, stat_send).wait()


def solution(mesh):
    tiles, dates = mesh.shape["tile"], mesh.shape["date"]
    nz = dates // NX

    def shards(secondary, primary, margin_mask, az_off, rg_off, az_frac, rg_frac):
        rows_n, cols_n = secondary.shape[2:]
        width = primary.shape[2]
        hbm = pl.BlockSpec(memory_space=pltpu.HBM)
        vmem = pl.BlockSpec(memory_space=pltpu.VMEM)
        dma = pltpu.SemaphoreType.DMA
        regular = pltpu.SemaphoreType.REGULAR
        chunks = cols_n // 128
        return pl.pallas_call(
            functools.partial(kernel, tiles, dates),
            out_shape=pltpu.VMEM((1, 2, rows_n // LA, cols_n // LR), F32),
            in_specs=[hbm] * 7,
            out_specs=vmem,
            scratch_shapes=[
                pltpu.VMEM((1, rows_n), jnp.int32),
                *[pltpu.VMEM((1, 1), jnp.int32)] * 2,
                *[pltpu.VMEM((1, 1), F32)] * 2,
                pltpu.VMEM((2, rows_n + 2 * RIM, cols_n), BF16),
                pltpu.VMEM((2 * width, rows_n), BF16),
                pltpu.VMEM((2 * rows_n, cols_n + 2 * SIDE), BF16),
                pltpu.VMEM((nz, NX, rows_n, 2 * width), BF16),
                pltpu.VMEM((chunks, 2 * rows_n, 128), BF16),
                pltpu.VMEM((chunks, 2 * rows_n, 128), F32),
                pltpu.VMEM((nz, NX, LAG, 2 * width), BF16),
                pltpu.VMEM((2, chunks, LAG, 128), BF16),
                pltpu.VMEM((1, 1, 128), F32),
                pltpu.VMEM((tiles - 1, 1, 128), F32),
                pltpu.VMEM((2 * rows_n, 128), F32),
                dma((7,)), dma((2,)), dma((2,)), dma((3,)), dma((3,)),
                dma((nz, NX - 1)), dma((nz, NX - 1)), dma((nz, NX)), dma((nz, NX)), dma((2,)), dma((2,)), dma, dma,
                regular((nz - 1,)), regular((NX - 1,)), regular, regular((len(ROUNDS),)),
            ],
            compiler_params=pltpu.CompilerParams(collective_id=0, has_side_effects=True),
            name="coregister",
        )(secondary, primary.transpose(0, 2, 1).reshape(2 * width, rows_n), margin_mask.reshape(1, rows_n), az_off, rg_off, az_frac, rg_frac)

    return jax.shard_map(
        shards,
        mesh=mesh,
        in_specs=(
            P("date", None, "tile", None),
            P(None, "tile", "date"),
            P("tile"),
            P("date", "tile"),
            P("date", "tile"),
            P("date", "tile"),
            P("date", "tile"),
        ),
        out_specs=P("date", None, "tile", None),
        check_vma=False,
    )
```

```python
import functools

import jax
import jax.numpy as jnp
from jax import lax
from jax.experimental import pallas as pl
from jax.experimental.pallas import tpu as pltpu
from jax.sharding import PartitionSpec as P

LAG = 64
LA = 2
LR = 8
NX = 4
RIM = 32
SIDE = 128
BLOCK = 256
MESH = pl.DeviceIdType.MESH
ROUNDS = (1, 2, 4, 8, 16)
F32 = jnp.float32
BF16 = jnp.bfloat16


def iota(shape, dim):
    return lax.broadcasted_iota(jnp.int32, shape, dim)


def tap_rows(frac, lanes):
    dist = iota((8, lanes), 0).astype(F32) - 3.0 - frac
    arg = jnp.pi * dist
    sinc = jnp.where(dist == 0.0, 1.0, jnp.sin(arg) / jnp.where(dist == 0.0, 1.0, arg))
    return sinc * (0.5 + 0.5 * jnp.cos(arg * 0.25))


def band(rows, first):
    total = jnp.zeros(first.shape, F32)
    for j in range(8):
        total = jnp.where(first == j - 3, rows[j : j + 1], total)
    return total.astype(BF16)


def kernel(
    tiles, dates,
    sec, prim, mask_at, az_off_at, rg_off_at, az_frac_at, rg_frac_at,
    out,
    mask, az_off, rg_off, az_frac, rg_frac,
    ext, prim_in, azim, gath, res, ifg, gnext, rnext, stat_out, stat_in, acc,
    local_sem, halo_send, halo_recv, z_send, z_recv, x_send, x_recv,
    next_send, next_recv, row_send, row_recv, stat_send, stat_recv,
    z_ready, x_ready, tile_ready, round_ready,
):
    nz = dates // NX
    rows_n = sec.shape[2]
    cols_n = sec.shape[3]
    width = prim.shape[0] // 2
    chunks = cols_n // 128
    t = lax.axis_index("tile")
    d = lax.axis_index("date")
    zh, x = d // NX, lax.rem(d, NX)

    def z_at(k):
        return lax.rem(zh + k + nz, nz)

    def date_at(z, xx):
        return z * NX + xx

    def remote(src, dst, ss, rs, tile, date):
        return pltpu.make_async_remote_copy(
            src_ref=src, dst_ref=dst, send_sem=ss, recv_sem=rs,
            device_id={"tile": tile, "date": date}, device_id_type=MESH,
        )

    def order(z):
        return jnp.where(z >= 2, 5 - z, z)

    def x_at(k):
        return lax.rem(x + k, NX)

    def signal(sem, tile, date):
        pl.semaphore_signal(sem, inc=1, device_id={"tile": tile, "date": date}, device_id_type=MESH)

    z_first = {k: order(zh) < order(z_at(k)) for k in range(1, nz)}
    x_first = {k: x < x_at(k) for k in range(1, NX)}
    barrier = pltpu.get_barrier_semaphore()
    for k in range(1, nz):
        @pl.when(z_first[k])
        def _(k=k):
            signal(barrier, t, date_at(z_at(k), x))
    for k in range(1, NX):
        @pl.when(x_first[k])
        def _(k=k):
            signal(barrier, t, date_at(zh, x_at(k)))

    @pl.when(t < tiles - 1)
    def _():
        signal(barrier, t + 1, d)

    small_copies = [
        pltpu.make_async_copy(src, dst, local_sem.at[2 + k])
        for k, (src, dst) in enumerate((
            (az_off_at, az_off), (rg_off_at, rg_off), (az_frac_at, az_frac), (rg_frac_at, rg_frac), (mask_at, mask),
        ))
    ]
    for copy in small_copies:
        copy.start()
    prim_copy = pltpu.make_async_copy(prim, prim_in, local_sem.at[0])
    prim_copy.start()
    own_copy = pltpu.make_async_copy(sec.at[0], ext.at[:, pl.ds(RIM, rows_n), :], local_sem.at[1])
    own_copy.start()

    @pl.when(t == 0)
    def _():
        ext[:, pl.ds(0, RIM), :] = jnp.zeros((2, RIM, cols_n), BF16)

    @pl.when(t == tiles - 1)
    def _():
        ext[:, pl.ds(RIM + rows_n, RIM), :] = jnp.zeros((2, RIM, cols_n), BF16)
        gnext[...] = jnp.zeros(gnext.shape, BF16)
        rnext[...] = jnp.zeros(rnext.shape, BF16)

    prim_copy.wait()
    mine = gath.at[zh, x]
    mine[...] = prim_in[...].astype(F32).T.astype(BF16)

    before = order(zh) + x + jnp.where(t > 0, 1, 0)

    @pl.when(before > 0)
    def _():
        pl.semaphore_wait(barrier, before)

    for k in (1, nz - 1):
        @pl.when(jnp.logical_not(z_first[k]))
        def _(k=k):
            signal(z_ready.at[nz - k - 1], t, date_at(z_at(k), x))
    for k in range(1, NX):
        @pl.when(jnp.logical_not(x_first[k]))
        def _(k=k):
            signal(x_ready.at[NX - k - 1], t, date_at(zh, x_at(k)))

    @pl.when(t > 0)
    def _():
        signal(tile_ready, t - 1, d)

    z_copies = {
        k: remote(mine, mine, z_send.at[k - 1], z_recv.at[nz - k - 1], t, date_at(z_at(k), x))
        for k in range(1, nz)
    }

    def x_copy(group, z, k):
        block = gath.at[z, x]
        return remote(block, block, x_send.at[group, k - 1], x_recv.at[group, k - 1], t, date_at(zh, x_at(k)))

    for k in (2, 1, 3):
        @pl.when(jnp.logical_not(z_first[k]))
        def _(k=k):
            z_copies[k].start()
    for k in (2, 1, 3):
        @pl.when(jnp.logical_not(x_first[k]))
        def _(k=k):
            x_copy(0, zh, k).start()

    up = remote(sec.at[0, :, pl.ds(rows_n - RIM, RIM), :], ext.at[:, pl.ds(0, RIM), :], halo_send.at[0], halo_recv.at[0], lax.rem(t + 1, tiles), d)
    down = remote(sec.at[0, :, pl.ds(0, RIM), :], ext.at[:, pl.ds(RIM + rows_n, RIM), :], halo_send.at[1], halo_recv.at[1], lax.rem(t + tiles - 1, tiles), d)

    @pl.when(t > 0)
    def _():
        down.start()

    for k in range(1, NX):
        @pl.when(x_first[k])
        def _(k=k):
            pl.semaphore_wait(x_ready.at[k - 1], 1)
            x_copy(0, zh, k).start()
            signal(x_ready.at[NX - k - 1], t, date_at(zh, x_at(k)))

    @pl.when(t < tiles - 1)
    def _():
        pl.semaphore_wait(tile_ready, 1)
        up.start()

    def round_signal(i):
        @pl.when(t >= ROUNDS[i])
        def _():
            signal(round_ready.at[i], t - ROUNDS[i], d)

        @pl.when(t < tiles - ROUNDS[i])
        def _():
            signal(round_ready.at[i], t + ROUNDS[i], d)

    def round_wait(i):
        expected = jnp.where(t >= ROUNDS[i], 1, 0) + jnp.where(t < tiles - ROUNDS[i], 1, 0)

        @pl.when(expected > 0)
        def _():
            pl.semaphore_wait(round_ready.at[i], expected)

    def next_copy(group, z, k):
        return remote(
            gath.at[z, x, pl.ds(0, LAG), :], gnext.at[z, x], next_send.at[group, k], next_recv.at[group, k],
            lax.rem(t + tiles - 1, tiles), date_at(zh, x_at(k)),
        )

    def spread_back(group, z):
        @pl.when(t > 0)
        def _():
            for k in (2, 1, 3, 0):
                next_copy(group, z, k).start()

    def spread(group, z):
        spread_back(group, z)
        for k in (2, 1, 3):
            x_copy(group, z, k).start()

    def turn(k):
        @pl.when(z_first[k])
        def _():
            pl.semaphore_wait(z_ready.at[k - 1], 1)
            z_copies[k].start()

    def arrive(k):
        block = gath.at[z_at(k), x]
        remote(block, block, z_send.at[k - 1], z_recv.at[k - 1], t, date_at(z_at(k), x)).wait_recv()
        spread(k, z_at(k))

    def pass_on(of, to):
        block = gath.at[z_at(of), x]
        return remote(block, block, z_send.at[1], z_recv.at[1], t, date_at(z_at(to), x))

    for k in range(1, NX):
        @pl.when(jnp.logical_not(x_first[k]))
        def _(k=k):
            pl.semaphore_wait(x_ready.at[k - 1], 1)
    spread_back(0, zh)

    round_signal(0)

    for copy in small_copies:
        copy.wait()
    az_rows = tap_rows(az_frac[...], 256)
    rg_rows = tap_rows(rg_frac[...], 256)
    span = rows_n + 2 * RIM
    az_taps = band(az_rows[:, :span], iota((rows_n, span), 1) - iota((rows_n, span), 0) - (az_off[...] + RIM))
    rg_shape = (BLOCK + 2 * SIDE, BLOCK)
    rg_taps = band(rg_rows, iota(rg_shape, 0) - iota(rg_shape, 1) - (rg_off[...] + SIDE))
    azim[:, pl.ds(0, SIDE)] = jnp.zeros((2 * rows_n, SIDE), BF16)
    azim[:, pl.ds(SIDE + cols_n, SIDE)] = jnp.zeros((2 * rows_n, SIDE), BF16)
    lanes = iota((1, mask.shape[1]), 1)
    marks = jnp.where(mask[...] != 0, 1.0, 0.0).astype(F32)
    picked = iota((LAG, mask.shape[1]), 1) == iota((LAG, mask.shape[1]), 0) + (rows_n - LAG)
    weight = jnp.sum(jnp.where(picked, marks, 0.0), axis=1, keepdims=True)
    count = jnp.sum(marks, axis=1, keepdims=True) * float(cols_n)

    own_copy.wait()

    @pl.when(t > 0)
    def _():
        up.wait_recv()

    @pl.when(t < tiles - 1)
    def _():
        down.wait_recv()

    for plane in range(2):
        for b in range(cols_n // BLOCK):
            part = jnp.dot(az_taps, ext[plane, :, pl.ds(b * BLOCK, BLOCK)], preferred_element_type=F32)
            azim[pl.ds(plane * rows_n, rows_n), pl.ds(SIDE + b * BLOCK, BLOCK)] = part.astype(BF16)

    round_wait(0)
    round_signal(1)

    for b in range(cols_n // BLOCK):
        part = jnp.dot(azim[:, pl.ds(b * BLOCK, BLOCK + 2 * SIDE)], rg_taps, preferred_element_type=F32).astype(BF16)
        for h in range(BLOCK // 128):
            half = part[:, h * 128 : (h + 1) * 128]
            res[b * (BLOCK // 128) + h] = half

    def row_copy(plane):
        return remote(
            res.at[:, pl.ds(plane * rows_n, LAG), :], rnext.at[plane], row_send.at[plane], row_recv.at[plane],
            lax.rem(t + tiles - 1, tiles), d,
        )

    round_wait(1)
    round_signal(2)

    @pl.when(t > 0)
    def _():
        row_copy(0).start()
        row_copy(1).start()

    turn(1)
    turn(3)
    arrive(1)

    @pl.when(zh == 0)
    def _():
        pass_on(1, 3).start()

    round_wait(2)
    round_signal(3)
    arrive(3)

    @pl.when(zh == 1)
    def _():
        pass_on(3, 1).start()

    round_wait(3)
    round_signal(4)
    arrive(2)

    @pl.when(t < tiles - 1)
    def _():
        row_copy(0).wait_recv()
        row_copy(1).wait_recv()

    low_half = iota((rows_n, 128), 1) < width

    def product(block_of, z, q, r_re, r_im, low):
        a = block_of[z, 2 * q].astype(F32)
        b = block_of[z, 2 * q + 1].astype(F32)
        p_re = jnp.where(low, a, pltpu.roll(b, width, 1))
        p_im = jnp.where(low, pltpu.roll(a, width, 1), b)
        return p_re * r_re + p_im * r_im, p_im * r_re - p_re * r_im

    def fold(v):
        return jnp.sum(v.reshape(LAG // 8, 8, 128), axis=0)

    def beat(group, z, sums):
        for k in range(1, NX):
            x_copy(group, z, k).wait_recv()

        @pl.when(t < tiles - 1)
        def _():
            for k in range(NX):
                next_copy(group, z, k).wait_recv()

        e_re, e_im, power = sums
        for q in range(NX // 2):
            m = z * (NX // 2) + q
            i_re, i_im = product(
                gath, z, q, res[m, pl.ds(0, rows_n)].astype(F32), res[m, pl.ds(rows_n, rows_n)].astype(F32), low_half
            )
            ifg[m, pl.ds(0, rows_n)] = i_re
            ifg[m, pl.ds(rows_n, rows_n)] = i_im
            l_re, l_im = product(gnext, z, q, rnext[0, m].astype(F32), rnext[1, m].astype(F32), low_half[:LAG])
            a_re, a_im = i_re[rows_n - LAG :], i_im[rows_n - LAG :]
            e_re += fold(weight * (a_re * l_re + a_im * l_im))
            e_im += fold(weight * (a_im * l_re - a_re * l_im))
            power += fold((0.5 * weight) * (a_re * a_re + a_im * a_im + l_re * l_re + l_im * l_im))
        return e_re, e_im, power

    zeros = jnp.zeros((8, 128), F32)
    sums = beat(0, zh, (zeros, zeros, zeros))
    sums = beat(1, z_at(1), sums)
    sums = beat(3, z_at(3), sums)
    round_wait(4)
    sums = beat(2, z_at(2), sums)

    lane = iota((1, 128), 1)
    own = jnp.where(lane == 3, count, 0.0)
    for k, v in enumerate(sums):
        own = jnp.where(lane == k, jnp.sum(jnp.sum(v, axis=0, keepdims=True), axis=1, keepdims=True), own)
    stat_out[0] = own

    def stat_copy(k):
        return remote(stat_out, stat_in.at[pl.ds(tiles - 1 - k, 1)], stat_send, stat_recv, lax.rem(t + k, tiles), d)

    for k in range(1, tiles):
        stat_copy(k).start()

    total = jnp.zeros((2 * rows_n, 128), F32)
    per = 128 // LR
    for m in range(chunks):
        pick = jnp.where(iota((128, 128), 1) == m * per + iota((128, 128), 0) // LR, 1.0 / (LA * LR), 0.0).astype(BF16)
        v = ifg[m]
        hi = v.astype(BF16)
        lo = (v - hi.astype(F32)).astype(BF16)
        total += jnp.dot(hi, pick, preferred_element_type=F32) + jnp.dot(lo, pick, preferred_element_type=F32)
    acc[...] = total
    pairs = [acc[pl.ds(first, rows_n, stride=LA), :] for first in range(LA)]
    both = functools.reduce(lambda a, b: a + b, pairs)
    looks_re, looks_im = both[: rows_n // LA], both[rows_n // LA :]

    pltpu.make_async_copy(stat_in, stat_in, stat_recv).wait()
    grand = own + jnp.sum(stat_in[...], axis=0)
    t_re, t_im, t_pow, t_cnt = (jnp.sum(jnp.where(lane == k, grand, 0.0), axis=1, keepdims=True) for k in range(4))
    magnitude = jnp.sqrt(t_re * t_re + t_im * t_im)
    floor_val = (t_pow + 1e-06) / jnp.sqrt(jnp.maximum(t_cnt, 1.0))
    denom = jnp.maximum(magnitude, floor_val)
    u_re = t_re / denom
    u_im = t_im / denom
    out[0, 0] = looks_re * u_re + looks_im * u_im
    out[0, 1] = looks_im * u_re - looks_re * u_im

    for k in range(1, nz):
        z_copies[k].wait_send()
    for group in range(nz):
        for k in range(1, NX):
            x_copy(group, z_at(group), k).wait_send()

    @pl.when(t < tiles - 1)
    def _():
        up.wait_send()

    @pl.when(t > 0)
    def _():
        down.wait_send()
        for group in range(nz):
            for k in range(NX):
                next_copy(group, z_at(group), k).wait_send()
        row_copy(0).wait_send()
        row_copy(1).wait_send()

    pltpu.make_async_copy(stat_in, stat_in, stat_send).wait()


def solution(mesh):
    tiles, dates = mesh.shape["tile"], mesh.shape["date"]
    nz = dates // NX

    def shards(secondary, primary, margin_mask, az_off, rg_off, az_frac, rg_frac):
        rows_n, cols_n = secondary.shape[2:]
        width = primary.shape[2]
        hbm = pl.BlockSpec(memory_space=pltpu.HBM)
        vmem = pl.BlockSpec(memory_space=pltpu.VMEM)
        dma = pltpu.SemaphoreType.DMA
        regular = pltpu.SemaphoreType.REGULAR
        chunks = cols_n // 128
        return pl.pallas_call(
            functools.partial(kernel, tiles, dates),
            out_shape=pltpu.VMEM((1, 2, rows_n // LA, cols_n // LR), F32),
            in_specs=[hbm] * 7,
            out_specs=vmem,
            scratch_shapes=[
                pltpu.VMEM((1, rows_n), jnp.int32),
                *[pltpu.VMEM((1, 1), jnp.int32)] * 2,
                *[pltpu.VMEM((1, 1), F32)] * 2,
                pltpu.VMEM((2, rows_n + 2 * RIM, cols_n), BF16),
                pltpu.VMEM((2 * width, rows_n), BF16),
                pltpu.VMEM((2 * rows_n, cols_n + 2 * SIDE), BF16),
                pltpu.VMEM((nz, NX, rows_n, 2 * width), BF16),
                pltpu.VMEM((chunks, 2 * rows_n, 128), BF16),
                pltpu.VMEM((chunks, 2 * rows_n, 128), F32),
                pltpu.VMEM((nz, NX, LAG, 2 * width), BF16),
                pltpu.VMEM((2, chunks, LAG, 128), BF16),
                pltpu.VMEM((1, 1, 128), F32),
                pltpu.VMEM((tiles - 1, 1, 128), F32),
                pltpu.VMEM((2 * rows_n, 128), F32),
                dma((7,)), dma((2,)), dma((2,)), dma((3,)), dma((3,)),
                dma((nz, NX - 1)), dma((nz, NX - 1)), dma((nz, NX)), dma((nz, NX)), dma((2,)), dma((2,)), dma, dma,
                regular((nz - 1,)), regular((NX - 1,)), regular, regular((len(ROUNDS),)),
            ],
            compiler_params=pltpu.CompilerParams(collective_id=0, has_side_effects=True),
            name="coregister",
        )(secondary, primary.transpose(0, 2, 1).reshape(2 * width, rows_n), margin_mask.reshape(1, rows_n), az_off, rg_off, az_frac, rg_frac)

    return jax.shard_map(
        shards,
        mesh=mesh,
        in_specs=(
            P("date", None, "tile", None),
            P(None, "tile", "date"),
            P("tile"),
            P("date", "tile"),
            P("date", "tile"),
            P("date", "tile"),
            P("date", "tile"),
        ),
        out_specs=P("date", None, "tile", None),
        check_vma=False,
    )
```

```python
import functools

import jax
import jax.numpy as jnp
from jax import lax
from jax.experimental import pallas as pl
from jax.experimental.pallas import tpu as pltpu
from jax.sharding import PartitionSpec as P

LAG = 64
LA = 2
LR = 8
NX = 4
RIM = 32
SIDE = 128
BLOCK = 256
MESH = pl.DeviceIdType.MESH
ROUNDS = (1, 2, 4, 8, 16)
F32 = jnp.float32
BF16 = jnp.bfloat16


def iota(shape, dim):
    return lax.broadcasted_iota(jnp.int32, shape, dim)


def tap_rows(frac, lanes):
    dist = iota((8, lanes), 0).astype(F32) - 3.0 - frac
    arg = jnp.pi * dist
    sinc = jnp.where(dist == 0.0, 1.0, jnp.sin(arg) / jnp.where(dist == 0.0, 1.0, arg))
    return sinc * (0.5 + 0.5 * jnp.cos(arg * 0.25))


def band(rows, first):
    total = jnp.zeros(first.shape, F32)
    for j in range(8):
        total = jnp.where(first == j - 3, rows[j : j + 1], total)
    return total.astype(BF16)


def kernel(
    tiles, dates,
    sec, prim, mask_at, az_off_at, rg_off_at, az_frac_at, rg_frac_at,
    out,
    mask, az_off, rg_off, az_frac, rg_frac,
    ext, prim_in, azim, gath, res, ifg, gnext, rnext, stat_out, stat_in, acc,
    local_sem, halo_send, halo_recv, z_send, z_recv, x_send, x_recv,
    next_send, next_recv, row_send, row_recv, stat_send, stat_recv,
    z_ready, x_ready, tile_ready, round_ready,
):
    nz = dates // NX
    rows_n = sec.shape[2]
    cols_n = sec.shape[3]
    width = prim.shape[0] // 2
    chunks = cols_n // 128
    t = lax.axis_index("tile")
    d = lax.axis_index("date")
    zh, x = d // NX, lax.rem(d, NX)

    def z_at(k):
        return lax.rem(zh + k + nz, nz)

    def date_at(z, xx):
        return z * NX + xx

    def remote(src, dst, ss, rs, tile, date):
        return pltpu.make_async_remote_copy(
            src_ref=src, dst_ref=dst, send_sem=ss, recv_sem=rs,
            device_id={"tile": tile, "date": date}, device_id_type=MESH,
        )

    def order(z):
        return jnp.where(z >= 2, 5 - z, z)

    def x_at(k):
        return lax.rem(x + k, NX)

    def signal(sem, tile, date):
        pl.semaphore_signal(sem, inc=1, device_id={"tile": tile, "date": date}, device_id_type=MESH)

    z_first = {k: order(zh) < order(z_at(k)) for k in (1, nz - 1)}
    x_first = {k: x < x_at(k) for k in range(1, NX)}
    barrier = pltpu.get_barrier_semaphore()
    @pl.when(zh == 0)
    def _():
        signal(barrier, t, date_at(z_at(2), x))

    for k in (1, nz - 1):
        @pl.when(z_first[k])
        def _(k=k):
            signal(barrier, t, date_at(z_at(k), x))
    for k in range(1, NX):
        @pl.when(x_first[k])
        def _(k=k):
            signal(barrier, t, date_at(zh, x_at(k)))

    @pl.when(t < tiles - 1)
    def _():
        signal(barrier, t + 1, d)

    small_copies = [
        pltpu.make_async_copy(src, dst, local_sem.at[2 + k])
        for k, (src, dst) in enumerate((
            (az_off_at, az_off), (rg_off_at, rg_off), (az_frac_at, az_frac), (rg_frac_at, rg_frac), (mask_at, mask),
        ))
    ]
    for copy in small_copies:
        copy.start()
    prim_copy = pltpu.make_async_copy(prim, prim_in, local_sem.at[0])
    prim_copy.start()
    own_copy = pltpu.make_async_copy(sec.at[0], ext.at[:, pl.ds(RIM, rows_n), :], local_sem.at[1])
    own_copy.start()

    @pl.when(t == 0)
    def _():
        ext[:, pl.ds(0, RIM), :] = jnp.zeros((2, RIM, cols_n), BF16)

    @pl.when(t == tiles - 1)
    def _():
        ext[:, pl.ds(RIM + rows_n, RIM), :] = jnp.zeros((2, RIM, cols_n), BF16)
        gnext[...] = jnp.zeros(gnext.shape, BF16)
        rnext[...] = jnp.zeros(rnext.shape, BF16)

    mine = gath.at[zh, x]

    before = sum(jnp.where(z_first[k], 0, 1) for k in (1, nz - 1)) + jnp.where(zh == 2, 1, 0) + x + jnp.where(t > 0, 1, 0)

    @pl.when(before > 0)
    def _():
        pl.semaphore_wait(barrier, before)

    for k in (1, nz - 1):
        @pl.when(jnp.logical_not(z_first[k]))
        def _(k=k):
            signal(z_ready.at[nz - k - 1], t, date_at(z_at(k), x))
    for k in range(1, NX):
        @pl.when(jnp.logical_not(x_first[k]))
        def _(k=k):
            signal(x_ready.at[NX - k - 1], t, date_at(zh, x_at(k)))

    @pl.when(t > 0)
    def _():
        signal(tile_ready, t - 1, d)

    up = remote(sec.at[0, :, pl.ds(rows_n - RIM, RIM), :], ext.at[:, pl.ds(0, RIM), :], halo_send.at[0], halo_recv.at[0], lax.rem(t + 1, tiles), d)
    down = remote(sec.at[0, :, pl.ds(0, RIM), :], ext.at[:, pl.ds(RIM + rows_n, RIM), :], halo_send.at[1], halo_recv.at[1], lax.rem(t + tiles - 1, tiles), d)

    @pl.when(t > 0)
    def _():
        down.start()

    prim_copy.wait()
    mine[...] = prim_in[...].astype(F32).T.astype(BF16)

    z_copies = {
        k: remote(mine, mine, z_send.at[k - 1], z_recv.at[nz - k - 1], t, date_at(z_at(k), x))
        for k in (1, nz - 1)
    }

    def x_copy(group, z, k):
        block = gath.at[z, x]
        return remote(block, block, x_send.at[group, k - 1], x_recv.at[group, k - 1], t, date_at(zh, x_at(k)))

    direct = remote(mine, mine, z_send.at[1], z_recv.at[1], t, date_at(z_at(2), x))

    @pl.when(zh == 2)
    def _():
        direct.start()

    for k in (1, nz - 1):
        @pl.when(jnp.logical_not(z_first[k]))
        def _(k=k):
            z_copies[k].start()
    for k in (2, 1, 3):
        @pl.when(jnp.logical_not(x_first[k]))
        def _(k=k):
            x_copy(0, zh, k).start()

    for k in range(1, NX):
        @pl.when(x_first[k])
        def _(k=k):
            pl.semaphore_wait(x_ready.at[k - 1], 1)
            x_copy(0, zh, k).start()
            signal(x_ready.at[NX - k - 1], t, date_at(zh, x_at(k)))

    @pl.when(t < tiles - 1)
    def _():
        pl.semaphore_wait(tile_ready, 1)
        up.start()

    def round_signal(i):
        @pl.when(t >= ROUNDS[i])
        def _():
            signal(round_ready.at[i], t - ROUNDS[i], d)

        @pl.when(t < tiles - ROUNDS[i])
        def _():
            signal(round_ready.at[i], t + ROUNDS[i], d)

    def round_wait(i):
        expected = jnp.where(t >= ROUNDS[i], 1, 0) + jnp.where(t < tiles - ROUNDS[i], 1, 0)

        @pl.when(expected > 0)
        def _():
            pl.semaphore_wait(round_ready.at[i], expected)

    def next_copy(group, z, k):
        return remote(
            gath.at[z, x, pl.ds(0, LAG), :], gnext.at[z, x], next_send.at[group, k], next_recv.at[group, k],
            lax.rem(t + tiles - 1, tiles), date_at(zh, x_at(k)),
        )

    def spread_back(group, z):
        @pl.when(t > 0)
        def _():
            for k in (2, 1, 3, 0):
                next_copy(group, z, k).start()

    def spread(group, z):
        spread_back(group, z)
        for k in (2, 1, 3):
            x_copy(group, z, k).start()

    def turn(k):
        @pl.when(z_first[k])
        def _():
            pl.semaphore_wait(z_ready.at[k - 1], 1)
            z_copies[k].start()

    def arrival(k):
        block = gath.at[z_at(k), x]
        remote(block, block, z_send.at[0], z_recv.at[k - 1], t, date_at(z_at(k), x)).wait_recv()

    near = jnp.where(zh == 0, 1, 3)
    far = nz - near

    def pass_on(of, to, sem):
        block = gath.at[z_at(of), x]
        return remote(block, block, z_send.at[sem], z_recv.at[1], t, date_at(z_at(to), x))

    passes = (
        (zh <= 1, pass_on(near, far, 1)),
        (zh == 0, pass_on(far, near, 3)),
    )

    round_signal(0)

    for copy in small_copies:
        copy.wait()
    az_rows = tap_rows(az_frac[...], 256)
    rg_rows = tap_rows(rg_frac[...], 256)
    span = rows_n + 2 * RIM
    az_taps = band(az_rows[:, :span], iota((rows_n, span), 1) - iota((rows_n, span), 0) - (az_off[...] + RIM))
    rg_shape = (BLOCK + 2 * SIDE, BLOCK)
    rg_taps = band(rg_rows, iota(rg_shape, 0) - iota(rg_shape, 1) - (rg_off[...] + SIDE))
    azim[:, pl.ds(0, SIDE)] = jnp.zeros((2 * rows_n, SIDE), BF16)
    azim[:, pl.ds(SIDE + cols_n, SIDE)] = jnp.zeros((2 * rows_n, SIDE), BF16)
    lanes = iota((1, mask.shape[1]), 1)
    marks = jnp.where(mask[...] != 0, 1.0, 0.0).astype(F32)
    picked = iota((LAG, mask.shape[1]), 1) == iota((LAG, mask.shape[1]), 0) + (rows_n - LAG)
    weight = jnp.sum(jnp.where(picked, marks, 0.0), axis=1, keepdims=True)
    count = jnp.sum(marks, axis=1, keepdims=True) * float(cols_n)

    round_wait(0)
    round_signal(1)
    turn(1)
    turn(3)
    own_copy.wait()

    @pl.when(t > 0)
    def _():
        up.wait_recv()

    @pl.when(t < tiles - 1)
    def _():
        down.wait_recv()

    for plane in range(2):
        for b in range(cols_n // BLOCK):
            part = jnp.dot(az_taps, ext[plane, :, pl.ds(b * BLOCK, BLOCK)], preferred_element_type=F32)
            azim[pl.ds(plane * rows_n, rows_n), pl.ds(SIDE + b * BLOCK, BLOCK)] = part.astype(BF16)


    for k in range(1, NX):
        @pl.when(jnp.logical_not(x_first[k]))
        def _(k=k):
            pl.semaphore_wait(x_ready.at[k - 1], 1)
    spread_back(0, zh)

    def take_near():
        arrival(near)

        @pl.when(passes[0][0])
        def _():
            passes[0][1].start()

        spread(near, z_at(near))

    @pl.when(zh != 2)
    def _():
        take_near()

    round_wait(1)
    round_signal(2)
    def row_copy(plane, b):
        piece = pl.ds(b * (BLOCK // 128), BLOCK // 128)
        return remote(
            res.at[piece, pl.ds(plane * rows_n, LAG), :], rnext.at[plane, piece], row_send.at[plane, b], row_recv.at[plane, b],
            lax.rem(t + tiles - 1, tiles), d,
        )

    def send_rows(b):
        @pl.when(t > 0)
        def _():
            row_copy(0, b).start()
            row_copy(1, b).start()

    for b in range(cols_n // BLOCK):
        part = jnp.dot(azim[:, pl.ds(b * BLOCK, BLOCK + 2 * SIDE)], rg_taps, preferred_element_type=F32).astype(BF16)
        for h in range(BLOCK // 128):
            half = part[:, h * 128 : (h + 1) * 128]
            res[b * (BLOCK // 128) + h] = half
        if b > 0:
            send_rows(b - 1)
    send_rows(cols_n // BLOCK - 1)


    round_wait(2)
    round_signal(3)
    @pl.when(zh == 2)
    def _():
        take_near()

    round_wait(3)
    round_signal(4)
    arrival(far)

    @pl.when(passes[1][0])
    def _():
        passes[1][1].start()

    spread(far, z_at(far))
    arrival(2)
    spread(2, z_at(2))

    @pl.when(t < tiles - 1)
    def _():
        for b in range(cols_n // BLOCK):
            for plane in range(2):
                row_copy(plane, b).wait_recv()

    low_half = iota((rows_n, 128), 1) < width

    def product(block_of, z, q, r_re, r_im, low):
        a = block_of[z, 2 * q].astype(F32)
        b = block_of[z, 2 * q + 1].astype(F32)
        p_re = jnp.where(low, a, pltpu.roll(b, width, 1))
        p_im = jnp.where(low, pltpu.roll(a, width, 1), b)
        return p_re * r_re + p_im * r_im, p_im * r_re - p_re * r_im

    def fold(v):
        return jnp.sum(v.reshape(LAG // 8, 8, 128), axis=0)

    def beat(group, z, sums):
        for k in range(1, NX):
            x_copy(group, z, k).wait_recv()

        @pl.when(t < tiles - 1)
        def _():
            for k in range(NX):
                next_copy(group, z, k).wait_recv()

        e_re, e_im, power = sums
        for q in range(NX // 2):
            m = z * (NX // 2) + q
            i_re, i_im = product(
                gath, z, q, res[m, pl.ds(0, rows_n)].astype(F32), res[m, pl.ds(rows_n, rows_n)].astype(F32), low_half
            )
            ifg[m, pl.ds(0, rows_n)] = i_re
            ifg[m, pl.ds(rows_n, rows_n)] = i_im
            l_re, l_im = product(gnext, z, q, rnext[0, m].astype(F32), rnext[1, m].astype(F32), low_half[:LAG])
            a_re, a_im = i_re[rows_n - LAG :], i_im[rows_n - LAG :]
            e_re += fold(weight * (a_re * l_re + a_im * l_im))
            e_im += fold(weight * (a_im * l_re - a_re * l_im))
            power += fold((0.5 * weight) * (a_re * a_re + a_im * a_im + l_re * l_re + l_im * l_im))
        return e_re, e_im, power

    zeros = jnp.zeros((8, 128), F32)
    sums = beat(0, zh, (zeros, zeros, zeros))
    sums = beat(1, z_at(1), sums)
    sums = beat(3, z_at(3), sums)
    round_wait(4)
    sums = beat(2, z_at(2), sums)

    lane = iota((1, 128), 1)
    own = jnp.where(lane == 3, count, 0.0)
    for k, v in enumerate(sums):
        own = jnp.where(lane == k, jnp.sum(jnp.sum(v, axis=0, keepdims=True), axis=1, keepdims=True), own)
    stat_out[0] = own

    def stat_copy(k):
        return remote(stat_out, stat_in.at[pl.ds(tiles - 1 - k, 1)], stat_send, stat_recv, lax.rem(t + k, tiles), d)

    for k in range(1, tiles):
        stat_copy(k).start()

    total = jnp.zeros((2 * rows_n, 128), F32)
    per = 128 // LR
    for m in range(chunks):
        pick = jnp.where(iota((128, 128), 1) == m * per + iota((128, 128), 0) // LR, 1.0 / (LA * LR), 0.0).astype(BF16)
        v = ifg[m]
        hi = v.astype(BF16)
        lo = (v - hi.astype(F32)).astype(BF16)
        total += jnp.dot(hi, pick, preferred_element_type=F32) + jnp.dot(lo, pick, preferred_element_type=F32)
    acc[...] = total
    pairs = [acc[pl.ds(first, rows_n, stride=LA), :] for first in range(LA)]
    both = functools.reduce(lambda a, b: a + b, pairs)
    looks_re, looks_im = both[: rows_n // LA], both[rows_n // LA :]

    pltpu.make_async_copy(stat_in, stat_in, stat_recv).wait()
    grand = own + jnp.sum(stat_in[...], axis=0)
    t_re, t_im, t_pow, t_cnt = (jnp.sum(jnp.where(lane == k, grand, 0.0), axis=1, keepdims=True) for k in range(4))
    magnitude = jnp.sqrt(t_re * t_re + t_im * t_im)
    floor_val = (t_pow + 1e-06) / jnp.sqrt(jnp.maximum(t_cnt, 1.0))
    denom = jnp.maximum(magnitude, floor_val)
    u_re = t_re / denom
    u_im = t_im / denom
    out[0, 0] = looks_re * u_re + looks_im * u_im
    out[0, 1] = looks_im * u_re - looks_re * u_im

    for copy in z_copies.values():
        copy.wait_send()

    @pl.when(zh == 2)
    def _():
        direct.wait_send()

    for here, copy in passes:
        @pl.when(here)
        def _(copy=copy):
            copy.wait_send()
    for group in range(nz):
        for k in range(1, NX):
            x_copy(group, z_at(group), k).wait_send()

    @pl.when(t < tiles - 1)
    def _():
        up.wait_send()

    @pl.when(t > 0)
    def _():
        down.wait_send()
        for group in range(nz):
            for k in range(NX):
                next_copy(group, z_at(group), k).wait_send()
        for b in range(cols_n // BLOCK):
            for plane in range(2):
                row_copy(plane, b).wait_send()

    pltpu.make_async_copy(stat_in, stat_in, stat_send).wait()


def solution(mesh):
    tiles, dates = mesh.shape["tile"], mesh.shape["date"]
    nz = dates // NX

    def shards(secondary, primary, margin_mask, az_off, rg_off, az_frac, rg_frac):
        rows_n, cols_n = secondary.shape[2:]
        width = primary.shape[2]
        hbm = pl.BlockSpec(memory_space=pltpu.HBM)
        vmem = pl.BlockSpec(memory_space=pltpu.VMEM)
        dma = pltpu.SemaphoreType.DMA
        regular = pltpu.SemaphoreType.REGULAR
        chunks = cols_n // 128
        return pl.pallas_call(
            functools.partial(kernel, tiles, dates),
            out_shape=pltpu.VMEM((1, 2, rows_n // LA, cols_n // LR), F32),
            in_specs=[hbm] * 7,
            out_specs=vmem,
            scratch_shapes=[
                pltpu.VMEM((1, rows_n), jnp.int32),
                *[pltpu.VMEM((1, 1), jnp.int32)] * 2,
                *[pltpu.VMEM((1, 1), F32)] * 2,
                pltpu.VMEM((2, rows_n + 2 * RIM, cols_n), BF16),
                pltpu.VMEM((2 * width, rows_n), BF16),
                pltpu.VMEM((2 * rows_n, cols_n + 2 * SIDE), BF16),
                pltpu.VMEM((nz, NX, rows_n, 2 * width), BF16),
                pltpu.VMEM((chunks, 2 * rows_n, 128), BF16),
                pltpu.VMEM((chunks, 2 * rows_n, 128), F32),
                pltpu.VMEM((nz, NX, LAG, 2 * width), BF16),
                pltpu.VMEM((2, chunks, LAG, 128), BF16),
                pltpu.VMEM((1, 1, 128), F32),
                pltpu.VMEM((tiles - 1, 1, 128), F32),
                pltpu.VMEM((2 * rows_n, 128), F32),
                dma((7,)), dma((2,)), dma((2,)), dma((4,)), dma((3,)),
                dma((nz, NX - 1)), dma((nz, NX - 1)), dma((nz, NX)), dma((nz, NX)), dma((2, cols_n // BLOCK)), dma((2, cols_n // BLOCK)), dma, dma,
                regular((nz - 1,)), regular((NX - 1,)), regular, regular((len(ROUNDS),)),
            ],
            compiler_params=pltpu.CompilerParams(collective_id=0, has_side_effects=True),
            name="coregister",
        )(secondary, primary.transpose(0, 2, 1).reshape(2 * width, rows_n), margin_mask.reshape(1, rows_n), az_off, rg_off, az_frac, rg_frac)

    return jax.shard_map(
        shards,
        mesh=mesh,
        in_specs=(
            P("date", None, "tile", None),
            P(None, "tile", "date"),
            P("tile"),
            P("date", "tile"),
            P("date", "tile"),
            P("date", "tile"),
            P("date", "tile"),
        ),
        out_specs=P("date", None, "tile", None),
        check_vma=False,
    )
```

```python
import functools

import jax
import jax.numpy as jnp
from jax import lax
from jax.experimental import pallas as pl
from jax.experimental.pallas import tpu as pltpu
from jax.sharding import PartitionSpec as P

LAG = 64
LA = 2
LR = 8
NX = 4
RIM = 32
SIDE = 128
BLOCK = 256
MESH = pl.DeviceIdType.MESH
ROUNDS = (1, 2, 4, 8, 16)
F32 = jnp.float32
BF16 = jnp.bfloat16


def iota(shape, dim):
    return lax.broadcasted_iota(jnp.int32, shape, dim)


def tap_rows(frac, lanes):
    dist = iota((8, lanes), 0).astype(F32) - 3.0 - frac
    arg = jnp.pi * dist
    sinc = jnp.where(dist == 0.0, 1.0, jnp.sin(arg) / jnp.where(dist == 0.0, 1.0, arg))
    return sinc * (0.5 + 0.5 * jnp.cos(arg * 0.25))


def band(rows, first):
    total = jnp.zeros(first.shape, F32)
    for j in range(8):
        total = jnp.where(first == j - 3, rows[j : j + 1], total)
    return total.astype(BF16)


def kernel(
    tiles, dates,
    sec, prim, mask_at, az_off_at, rg_off_at, az_frac_at, rg_frac_at,
    out,
    mask, az_off, rg_off, az_frac, rg_frac,
    ext, prim_in, azim, gath, res, ifg, gnext, rnext, stat_out, stat_in, acc,
    local_sem, halo_send, halo_recv, z_send, z_recv, x_send, x_recv,
    next_send, next_recv, row_send, row_recv, stat_send, stat_recv,
    z_ready, x_ready, tile_ready, round_ready,
):
    prim_copy = pltpu.make_async_copy(prim, prim_in, local_sem.at[0])
    prim_copy.start()
    nz = dates // NX
    rows_n = sec.shape[2]
    cols_n = sec.shape[3]
    width = prim.shape[0] // 2
    chunks = cols_n // 128
    t = lax.axis_index("tile")
    d = lax.axis_index("date")
    zh, x = d // NX, lax.rem(d, NX)

    def z_at(k):
        return lax.rem(zh + k + nz, nz)

    def date_at(z, xx):
        return z * NX + xx

    def remote(src, dst, ss, rs, tile, date):
        return pltpu.make_async_remote_copy(
            src_ref=src, dst_ref=dst, send_sem=ss, recv_sem=rs,
            device_id={"tile": tile, "date": date}, device_id_type=MESH,
        )

    def order(z):
        return jnp.where(z >= 2, 5 - z, z)

    def x_at(k):
        return lax.rem(x + k, NX)

    def signal(sem, tile, date):
        pl.semaphore_signal(sem, inc=1, device_id={"tile": tile, "date": date}, device_id_type=MESH)

    z_first = {k: order(zh) < order(z_at(k)) for k in (1, nz - 1)}
    x_first = {k: x < x_at(k) for k in range(1, NX)}
    barrier = pltpu.get_barrier_semaphore()
    @pl.when(zh == 0)
    def _():
        signal(barrier, t, date_at(z_at(2), x))

    for k in (1, nz - 1):
        @pl.when(z_first[k])
        def _(k=k):
            signal(barrier, t, date_at(z_at(k), x))
    for k in range(1, NX):
        @pl.when(x_first[k])
        def _(k=k):
            signal(barrier, t, date_at(zh, x_at(k)))

    @pl.when(t < tiles - 1)
    def _():
        signal(barrier, t + 1, d)

    small_copies = [
        pltpu.make_async_copy(src, dst, local_sem.at[2 + k])
        for k, (src, dst) in enumerate((
            (az_off_at, az_off), (rg_off_at, rg_off), (az_frac_at, az_frac), (rg_frac_at, rg_frac), (mask_at, mask),
        ))
    ]
    for copy in small_copies:
        copy.start()
    own_copy = pltpu.make_async_copy(sec.at[0], ext.at[:, pl.ds(RIM, rows_n), :], local_sem.at[1])
    own_copy.start()

    mine = gath.at[zh, x]

    before = sum(jnp.where(z_first[k], 0, 1) for k in (1, nz - 1)) + jnp.where(zh == 2, 1, 0) + x + jnp.where(t > 0, 1, 0)

    @pl.when(before > 0)
    def _():
        pl.semaphore_wait(barrier, before)

    for k in (1, nz - 1):
        @pl.when(jnp.logical_not(z_first[k]))
        def _(k=k):
            signal(z_ready.at[nz - k - 1], t, date_at(z_at(k), x))
    for k in range(1, NX):
        @pl.when(jnp.logical_not(x_first[k]))
        def _(k=k):
            signal(x_ready.at[NX - k - 1], t, date_at(zh, x_at(k)))

    @pl.when(t > 0)
    def _():
        signal(tile_ready, t - 1, d)

    prim_copy.wait()
    mine[...] = prim_in[...].astype(F32).T.astype(BF16)

    z_copies = {
        k: remote(mine, mine, z_send.at[k - 1], z_recv.at[nz - k - 1], t, date_at(z_at(k), x))
        for k in (1, nz - 1)
    }

    def x_copy(group, z, k):
        block = gath.at[z, x]
        return remote(block, block, x_send.at[group, k - 1], x_recv.at[group, k - 1], t, date_at(zh, x_at(k)))

    direct = remote(mine, mine, z_send.at[1], z_recv.at[1], t, date_at(z_at(2), x))

    @pl.when(zh == 2)
    def _():
        direct.start()

    for k in (1, nz - 1):
        @pl.when(jnp.logical_not(z_first[k]) & (zh != 2))
        def _(k=k):
            z_copies[k].start()
    for k in (2, 1, 3):
        @pl.when(jnp.logical_not(x_first[k]))
        def _(k=k):
            x_copy(0, zh, k).start()

    up = remote(sec.at[0, :, pl.ds(rows_n - RIM, RIM), :], ext.at[:, pl.ds(0, RIM), :], halo_send.at[0], halo_recv.at[0], lax.rem(t + 1, tiles), d)
    down = remote(sec.at[0, :, pl.ds(0, RIM), :], ext.at[:, pl.ds(RIM + rows_n, RIM), :], halo_send.at[1], halo_recv.at[1], lax.rem(t + tiles - 1, tiles), d)

    @pl.when(t > 0)
    def _():
        down.start()

    for k in range(1, NX):
        @pl.when(x_first[k])
        def _(k=k):
            pl.semaphore_wait(x_ready.at[k - 1], 1)
            x_copy(0, zh, k).start()
            signal(x_ready.at[NX - k - 1], t, date_at(zh, x_at(k)))

    @pl.when(t < tiles - 1)
    def _():
        pl.semaphore_wait(tile_ready, 1)
        up.start()

    @pl.when(zh == 2)
    def _():
        z_copies[1].start()
        z_copies[3].start()

    def round_signal(i):
        @pl.when(t >= ROUNDS[i])
        def _():
            signal(round_ready.at[i], t - ROUNDS[i], d)

        @pl.when(t < tiles - ROUNDS[i])
        def _():
            signal(round_ready.at[i], t + ROUNDS[i], d)

    def round_wait(i):
        expected = jnp.where(t >= ROUNDS[i], 1, 0) + jnp.where(t < tiles - ROUNDS[i], 1, 0)

        @pl.when(expected > 0)
        def _():
            pl.semaphore_wait(round_ready.at[i], expected)

    def next_copy(group, z, k):
        return remote(
            gath.at[z, x, pl.ds(0, LAG), :], gnext.at[z, x], next_send.at[group, k], next_recv.at[group, k],
            lax.rem(t + tiles - 1, tiles), date_at(zh, x_at(k)),
        )

    def spread_back(group, z):
        @pl.when(t > 0)
        def _():
            for k in (2, 1, 3, 0):
                next_copy(group, z, k).start()

    def spread(group, z):
        spread_back(group, z)
        for k in (2, 1, 3):
            x_copy(group, z, k).start()

    def turn(k):
        @pl.when(z_first[k])
        def _():
            pl.semaphore_wait(z_ready.at[k - 1], 1)
            z_copies[k].start()

    def arrival(k):
        block = gath.at[z_at(k), x]
        remote(block, block, z_send.at[0], z_recv.at[k - 1], t, date_at(z_at(k), x)).wait_recv()

    near = jnp.where(zh == 0, 1, 3)
    far = nz - near

    def pass_on(of, to, sem):
        block = gath.at[z_at(of), x]
        return remote(block, block, z_send.at[sem], z_recv.at[1], t, date_at(z_at(to), x))

    passes = (
        (zh <= 1, pass_on(near, far, 1)),
        (zh == 0, pass_on(far, near, 3)),
    )

    round_signal(0)

    @pl.when(t == 0)
    def _():
        ext[:, pl.ds(0, RIM), :] = jnp.zeros((2, RIM, cols_n), BF16)

    @pl.when(t == tiles - 1)
    def _():
        ext[:, pl.ds(RIM + rows_n, RIM), :] = jnp.zeros((2, RIM, cols_n), BF16)
        gnext[...] = jnp.zeros(gnext.shape, BF16)
        rnext[...] = jnp.zeros(rnext.shape, BF16)

    for copy in small_copies:
        copy.wait()
    az_rows = tap_rows(az_frac[...], 256)
    rg_rows = tap_rows(rg_frac[...], 256)
    span = rows_n + 2 * RIM
    az_taps = band(az_rows[:, :span], iota((rows_n, span), 1) - iota((rows_n, span), 0) - (az_off[...] + RIM))
    rg_shape = (BLOCK + 2 * SIDE, BLOCK)
    rg_taps = band(rg_rows, iota(rg_shape, 0) - iota(rg_shape, 1) - (rg_off[...] + SIDE))
    azim[:, pl.ds(0, SIDE)] = jnp.zeros((2 * rows_n, SIDE), BF16)
    azim[:, pl.ds(SIDE + cols_n, SIDE)] = jnp.zeros((2 * rows_n, SIDE), BF16)
    lanes = iota((1, mask.shape[1]), 1)
    marks = jnp.where(mask[...] != 0, 1.0, 0.0).astype(F32)
    picked = iota((LAG, mask.shape[1]), 1) == iota((LAG, mask.shape[1]), 0) + (rows_n - LAG)
    weight = jnp.sum(jnp.where(picked, marks, 0.0), axis=1, keepdims=True)
    count = jnp.sum(marks, axis=1, keepdims=True) * float(cols_n)

    round_wait(0)
    round_signal(1)
    turn(1)
    turn(3)
    own_copy.wait()

    @pl.when(t > 0)
    def _():
        up.wait_recv()

    @pl.when(t < tiles - 1)
    def _():
        down.wait_recv()

    for plane in range(2):
        for b in range(cols_n // BLOCK):
            part = jnp.dot(az_taps, ext[plane, :, pl.ds(b * BLOCK, BLOCK)], preferred_element_type=F32)
            azim[pl.ds(plane * rows_n, rows_n), pl.ds(SIDE + b * BLOCK, BLOCK)] = part.astype(BF16)


    for k in range(1, NX):
        @pl.when(jnp.logical_not(x_first[k]))
        def _(k=k):
            pl.semaphore_wait(x_ready.at[k - 1], 1)
    spread_back(0, zh)

    def take_near():
        arrival(near)

        @pl.when(passes[0][0])
        def _():
            passes[0][1].start()

        spread(near, z_at(near))

    @pl.when(zh != 2)
    def _():
        take_near()

    round_wait(1)
    round_signal(2)
    def row_copy(plane, b):
        piece = pl.ds(b * (BLOCK // 128), BLOCK // 128)
        return remote(
            res.at[piece, pl.ds(plane * rows_n, LAG), :], rnext.at[plane, piece], row_send.at[plane, b], row_recv.at[plane, b],
            lax.rem(t + tiles - 1, tiles), d,
        )

    def send_rows(b):
        @pl.when(t > 0)
        def _():
            row_copy(0, b).start()
            row_copy(1, b).start()

    for b in range(cols_n // BLOCK):
        part = jnp.dot(azim[:, pl.ds(b * BLOCK, BLOCK + 2 * SIDE)], rg_taps, preferred_element_type=F32).astype(BF16)
        for h in range(BLOCK // 128):
            half = part[:, h * 128 : (h + 1) * 128]
            res[b * (BLOCK // 128) + h] = half
        if b > 0:
            send_rows(b - 1)
    send_rows(cols_n // BLOCK - 1)


    round_wait(2)
    round_signal(3)
    @pl.when(zh == 2)
    def _():
        take_near()

    round_wait(3)
    round_signal(4)
    arrival(far)

    @pl.when(passes[1][0])
    def _():
        passes[1][1].start()

    spread(far, z_at(far))
    arrival(2)
    spread(2, z_at(2))

    @pl.when(t < tiles - 1)
    def _():
        for b in range(cols_n // BLOCK):
            for plane in range(2):
                row_copy(plane, b).wait_recv()

    low_half = iota((rows_n, 128), 1) < width

    def product(block_of, z, q, r_re, r_im, low):
        a = block_of[z, 2 * q].astype(F32)
        b = block_of[z, 2 * q + 1].astype(F32)
        p_re = jnp.where(low, a, pltpu.roll(b, width, 1))
        p_im = jnp.where(low, pltpu.roll(a, width, 1), b)
        return p_re * r_re + p_im * r_im, p_im * r_re - p_re * r_im

    def fold(v):
        return jnp.sum(v.reshape(LAG // 8, 8, 128), axis=0)

    def beat(group, z, sums):
        for k in range(1, NX):
            x_copy(group, z, k).wait_recv()

        @pl.when(t < tiles - 1)
        def _():
            for k in range(NX):
                next_copy(group, z, k).wait_recv()

        e_re, e_im, power = sums
        for q in range(NX // 2):
            m = z * (NX // 2) + q
            i_re, i_im = product(
                gath, z, q, res[m, pl.ds(0, rows_n)].astype(F32), res[m, pl.ds(rows_n, rows_n)].astype(F32), low_half
            )
            ifg[m, pl.ds(0, rows_n)] = i_re
            ifg[m, pl.ds(rows_n, rows_n)] = i_im
            l_re, l_im = product(gnext, z, q, rnext[0, m].astype(F32), rnext[1, m].astype(F32), low_half[:LAG])
            a_re, a_im = i_re[rows_n - LAG :], i_im[rows_n - LAG :]
            e_re += fold(weight * (a_re * l_re + a_im * l_im))
            e_im += fold(weight * (a_im * l_re - a_re * l_im))
            power += fold((0.5 * weight) * (a_re * a_re + a_im * a_im + l_re * l_re + l_im * l_im))
        return e_re, e_im, power

    zeros = jnp.zeros((8, 128), F32)
    sums = beat(0, zh, (zeros, zeros, zeros))
    sums = beat(1, z_at(1), sums)
    sums = beat(3, z_at(3), sums)
    round_wait(4)
    sums = beat(2, z_at(2), sums)

    lane = iota((1, 128), 1)
    own = jnp.where(lane == 3, count, 0.0)
    for k, v in enumerate(sums):
        own = jnp.where(lane == k, jnp.sum(jnp.sum(v, axis=0, keepdims=True), axis=1, keepdims=True), own)
    stat_out[0] = own

    zl, y, core = t // 8, lax.rem(t // 2, 4), lax.rem(t, 2)
    offsets = [(dz, dy, dc) for dy in (2, 1, 3, 0) for dz in (3, 1, 2, 0) for dc in (1, 0)][: tiles - 1]

    def stat_copy(i):
        dz, dy, dc = offsets[i]
        tile = lax.rem(zl + dz, 4) * 8 + lax.rem(y + dy, 4) * 2 + lax.rem(core + dc, 2)
        return remote(stat_out, stat_in.at[pl.ds(i, 1)], stat_send, stat_recv, tile, d)

    for i in range(tiles - 1):
        stat_copy(i).start()

    total = jnp.zeros((2 * rows_n, 128), F32)
    per = 128 // LR
    for m in range(chunks):
        pick = jnp.where(iota((128, 128), 1) == m * per + iota((128, 128), 0) // LR, 1.0 / (LA * LR), 0.0).astype(BF16)
        v = ifg[m]
        hi = v.astype(BF16)
        lo = (v - hi.astype(F32)).astype(BF16)
        total += jnp.dot(hi, pick, preferred_element_type=F32) + jnp.dot(lo, pick, preferred_element_type=F32)
    acc[...] = total
    pairs = [acc[pl.ds(first, rows_n, stride=LA), :] for first in range(LA)]
    both = functools.reduce(lambda a, b: a + b, pairs)
    looks_re, looks_im = both[: rows_n // LA], both[rows_n // LA :]

    pltpu.make_async_copy(stat_in, stat_in, stat_recv).wait()
    grand = own + jnp.sum(stat_in[...], axis=0)
    t_re, t_im, t_pow, t_cnt = (jnp.sum(jnp.where(lane == k, grand, 0.0), axis=1, keepdims=True) for k in range(4))
    magnitude = jnp.sqrt(t_re * t_re + t_im * t_im)
    floor_val = (t_pow + 1e-06) / jnp.sqrt(jnp.maximum(t_cnt, 1.0))
    denom = jnp.maximum(magnitude, floor_val)
    u_re = t_re / denom
    u_im = t_im / denom
    out[0, 0] = looks_re * u_re + looks_im * u_im
    out[0, 1] = looks_im * u_re - looks_re * u_im

    for copy in z_copies.values():
        copy.wait_send()

    @pl.when(zh == 2)
    def _():
        direct.wait_send()

    for here, copy in passes:
        @pl.when(here)
        def _(copy=copy):
            copy.wait_send()
    for group in range(nz):
        for k in range(1, NX):
            x_copy(group, z_at(group), k).wait_send()

    @pl.when(t < tiles - 1)
    def _():
        up.wait_send()

    @pl.when(t > 0)
    def _():
        down.wait_send()
        for group in range(nz):
            for k in range(NX):
                next_copy(group, z_at(group), k).wait_send()
        for b in range(cols_n // BLOCK):
            for plane in range(2):
                row_copy(plane, b).wait_send()

    pltpu.make_async_copy(stat_in, stat_in, stat_send).wait()


def solution(mesh):
    tiles, dates = mesh.shape["tile"], mesh.shape["date"]
    nz = dates // NX

    def shards(secondary, primary, margin_mask, az_off, rg_off, az_frac, rg_frac):
        rows_n, cols_n = secondary.shape[2:]
        width = primary.shape[2]
        hbm = pl.BlockSpec(memory_space=pltpu.HBM)
        vmem = pl.BlockSpec(memory_space=pltpu.VMEM)
        dma = pltpu.SemaphoreType.DMA
        regular = pltpu.SemaphoreType.REGULAR
        chunks = cols_n // 128
        return pl.pallas_call(
            functools.partial(kernel, tiles, dates),
            out_shape=pltpu.VMEM((1, 2, rows_n // LA, cols_n // LR), F32),
            in_specs=[hbm] * 7,
            out_specs=vmem,
            scratch_shapes=[
                pltpu.VMEM((1, rows_n), jnp.int32),
                *[pltpu.VMEM((1, 1), jnp.int32)] * 2,
                *[pltpu.VMEM((1, 1), F32)] * 2,
                pltpu.VMEM((2, rows_n + 2 * RIM, cols_n), BF16),
                pltpu.VMEM((2 * width, rows_n), BF16),
                pltpu.VMEM((2 * rows_n, cols_n + 2 * SIDE), BF16),
                pltpu.VMEM((nz, NX, rows_n, 2 * width), BF16),
                pltpu.VMEM((chunks, 2 * rows_n, 128), BF16),
                pltpu.VMEM((chunks, 2 * rows_n, 128), F32),
                pltpu.VMEM((nz, NX, LAG, 2 * width), BF16),
                pltpu.VMEM((2, chunks, LAG, 128), BF16),
                pltpu.VMEM((1, 1, 128), F32),
                pltpu.VMEM((tiles - 1, 1, 128), F32),
                pltpu.VMEM((2 * rows_n, 128), F32),
                dma((7,)), dma((2,)), dma((2,)), dma((4,)), dma((3,)),
                dma((nz, NX - 1)), dma((nz, NX - 1)), dma((nz, NX)), dma((nz, NX)), dma((2, cols_n // BLOCK)), dma((2, cols_n // BLOCK)), dma, dma,
                regular((nz - 1,)), regular((NX - 1,)), regular, regular((len(ROUNDS),)),
            ],
            compiler_params=pltpu.CompilerParams(collective_id=0, has_side_effects=True),
            name="coregister",
        )(secondary, primary.transpose(0, 2, 1).reshape(2 * width, rows_n), margin_mask.reshape(1, rows_n), az_off, rg_off, az_frac, rg_frac)

    return jax.shard_map(
        shards,
        mesh=mesh,
        in_specs=(
            P("date", None, "tile", None),
            P(None, "tile", "date"),
            P("tile"),
            P("date", "tile"),
            P("date", "tile"),
            P("date", "tile"),
            P("date", "tile"),
        ),
        out_specs=P("date", None, "tile", None),
        check_vma=False,
    )
```

```python
import functools

import jax
import jax.numpy as jnp
from jax import lax
from jax.experimental import pallas as pl
from jax.experimental.pallas import tpu as pltpu
from jax.sharding import PartitionSpec as P

LAG = 64
LA = 2
LR = 8
NX = 4
RIM = 32
SIDE = 128
BLOCK = 256
MESH = pl.DeviceIdType.MESH
ROUNDS = (1, 2, 4, 8, 16)
F32 = jnp.float32
BF16 = jnp.bfloat16


def iota(shape, dim):
    return lax.broadcasted_iota(jnp.int32, shape, dim)


def tap_rows(frac, lanes):
    dist = iota((8, lanes), 0).astype(F32) - 3.0 - frac
    arg = jnp.pi * dist
    sinc = jnp.where(dist == 0.0, 1.0, jnp.sin(arg) / jnp.where(dist == 0.0, 1.0, arg))
    return sinc * (0.5 + 0.5 * jnp.cos(arg * 0.25))


def band(rows, first):
    total = jnp.zeros(first.shape, F32)
    for j in range(8):
        total = jnp.where(first == j - 3, rows[j : j + 1], total)
    return total.astype(BF16)


def kernel(
    tiles, dates,
    sec, prim, mask_at, az_off_at, rg_off_at, az_frac_at, rg_frac_at,
    out,
    mask, az_off, rg_off, az_frac, rg_frac,
    ext, prim_in, azim, gath, res, ifg, gnext, rnext, stat_out, stat_in, acc,
    local_sem, halo_send, halo_recv, z_send, z_recv, x_send, x_recv,
    next_send, next_recv, row_send, row_recv, stat_send, stat_recv,
    z_ready, x_ready, tile_ready, round_ready,
):
    prim_copy = pltpu.make_async_copy(prim, prim_in, local_sem.at[0])
    prim_copy.start()
    nz = dates // NX
    rows_n = sec.shape[2]
    cols_n = sec.shape[3]
    width = prim.shape[0] // 2
    chunks = cols_n // 128
    t = lax.axis_index("tile")
    d = lax.axis_index("date")
    zh, x = d // NX, lax.rem(d, NX)

    def z_at(k):
        return lax.rem(zh + k + nz, nz)

    def date_at(z, xx):
        return z * NX + xx

    def remote(src, dst, ss, rs, tile, date):
        return pltpu.make_async_remote_copy(
            src_ref=src, dst_ref=dst, send_sem=ss, recv_sem=rs,
            device_id={"tile": tile, "date": date}, device_id_type=MESH,
        )

    def order(z):
        return jnp.where(z >= 2, 5 - z, z)

    def x_at(k):
        return lax.rem(x + k, NX)

    def signal(sem, tile, date):
        pl.semaphore_signal(sem, inc=1, device_id={"tile": tile, "date": date}, device_id_type=MESH)

    z_first = {k: order(zh) < order(z_at(k)) for k in (1, nz - 1)}
    x_first = {k: x < x_at(k) for k in range(1, NX)}
    barrier = pltpu.get_barrier_semaphore()
    @pl.when(zh == 0)
    def _():
        signal(barrier, t, date_at(z_at(2), x))

    for k in (1, nz - 1):
        @pl.when(z_first[k])
        def _(k=k):
            signal(barrier, t, date_at(z_at(k), x))
    for k in range(1, NX):
        @pl.when(x_first[k])
        def _(k=k):
            signal(barrier, t, date_at(zh, x_at(k)))

    @pl.when(t < tiles - 1)
    def _():
        signal(barrier, t + 1, d)

    small_copies = [
        pltpu.make_async_copy(src, dst, local_sem.at[2 + k])
        for k, (src, dst) in enumerate((
            (az_off_at, az_off), (rg_off_at, rg_off), (az_frac_at, az_frac), (rg_frac_at, rg_frac), (mask_at, mask),
        ))
    ]
    for copy in small_copies:
        copy.start()
    own_copy = pltpu.make_async_copy(sec.at[0], ext.at[:, pl.ds(RIM, rows_n), :], local_sem.at[1])
    own_copy.start()

    mine = gath.at[zh, x]

    before = sum(jnp.where(z_first[k], 0, 1) for k in (1, nz - 1)) + jnp.where(zh == 2, 1, 0) + x + jnp.where(t > 0, 1, 0)

    @pl.when(before > 0)
    def _():
        pl.semaphore_wait(barrier, before)

    for k in (1, nz - 1):
        @pl.when(jnp.logical_not(z_first[k]))
        def _(k=k):
            signal(z_ready.at[nz - k - 1], t, date_at(z_at(k), x))
    for k in range(1, NX):
        @pl.when(jnp.logical_not(x_first[k]))
        def _(k=k):
            signal(x_ready.at[NX - k - 1], t, date_at(zh, x_at(k)))

    @pl.when(t > 0)
    def _():
        signal(tile_ready, t - 1, d)

    prim_copy.wait()
    mine[...] = prim_in[...].astype(F32).T.astype(BF16)

    z_copies = {
        k: remote(mine, mine, z_send.at[k - 1], z_recv.at[nz - k - 1], t, date_at(z_at(k), x))
        for k in (1, nz - 1)
    }

    def x_copy(group, z, k):
        block = gath.at[z, x]
        return remote(block, block, x_send.at[group, k - 1], x_recv.at[group, k - 1], t, date_at(zh, x_at(k)))

    direct = remote(mine, mine, z_send.at[1], z_recv.at[1], t, date_at(z_at(2), x))

    @pl.when(zh == 2)
    def _():
        direct.start()

    for k in (1, nz - 1):
        @pl.when(jnp.logical_not(z_first[k]) & (zh != 2))
        def _(k=k):
            z_copies[k].start()
    for k in (2, 1, 3):
        @pl.when(jnp.logical_not(x_first[k]))
        def _(k=k):
            x_copy(0, zh, k).start()

    up = remote(sec.at[0, :, pl.ds(rows_n - RIM, RIM), :], ext.at[:, pl.ds(0, RIM), :], halo_send.at[0], halo_recv.at[0], lax.rem(t + 1, tiles), d)
    down = remote(sec.at[0, :, pl.ds(0, RIM), :], ext.at[:, pl.ds(RIM + rows_n, RIM), :], halo_send.at[1], halo_recv.at[1], lax.rem(t + tiles - 1, tiles), d)

    @pl.when(t > 0)
    def _():
        down.start()

    for k in range(1, NX):
        @pl.when(x_first[k])
        def _(k=k):
            pl.semaphore_wait(x_ready.at[k - 1], 1)
            x_copy(0, zh, k).start()
            signal(x_ready.at[NX - k - 1], t, date_at(zh, x_at(k)))

    @pl.when(t < tiles - 1)
    def _():
        pl.semaphore_wait(tile_ready, 1)
        up.start()

    @pl.when(zh == 2)
    def _():
        z_copies[1].start()
        z_copies[3].start()

    def round_signal(i):
        @pl.when(t >= ROUNDS[i])
        def _():
            signal(round_ready.at[i], t - ROUNDS[i], d)

        @pl.when(t < tiles - ROUNDS[i])
        def _():
            signal(round_ready.at[i], t + ROUNDS[i], d)

    def round_wait(i):
        expected = jnp.where(t >= ROUNDS[i], 1, 0) + jnp.where(t < tiles - ROUNDS[i], 1, 0)

        @pl.when(expected > 0)
        def _():
            pl.semaphore_wait(round_ready.at[i], expected)

    def next_copy(group, z, k):
        return remote(
            gath.at[z, x, pl.ds(0, LAG), :], gnext.at[z, x], next_send.at[group, k], next_recv.at[group, k],
            lax.rem(t + tiles - 1, tiles), date_at(zh, x_at(k)),
        )

    def spread_back(group, z):
        @pl.when(t > 0)
        def _():
            for k in (2, 1, 3, 0):
                next_copy(group, z, k).start()

    def spread(group, z):
        spread_back(group, z)
        for k in (2, 1, 3):
            x_copy(group, z, k).start()

    def turn(k):
        @pl.when(z_first[k])
        def _():
            pl.semaphore_wait(z_ready.at[k - 1], 1)
            z_copies[k].start()

    def arrival(k):
        block = gath.at[z_at(k), x]
        remote(block, block, z_send.at[0], z_recv.at[k - 1], t, date_at(z_at(k), x)).wait_recv()

    near = jnp.where(zh == 0, 1, 3)
    far = nz - near

    def pass_on(of, to, sem):
        block = gath.at[z_at(of), x]
        return remote(block, block, z_send.at[sem], z_recv.at[1], t, date_at(z_at(to), x))

    passes = (
        (zh <= 1, pass_on(near, far, 1)),
        (zh == 0, pass_on(far, near, 3)),
    )

    round_signal(0)

    @pl.when(t == 0)
    def _():
        ext[:, pl.ds(0, RIM), :] = jnp.zeros((2, RIM, cols_n), BF16)

    @pl.when(t == tiles - 1)
    def _():
        ext[:, pl.ds(RIM + rows_n, RIM), :] = jnp.zeros((2, RIM, cols_n), BF16)
        gnext[...] = jnp.zeros(gnext.shape, BF16)
        rnext[...] = jnp.zeros(rnext.shape, BF16)

    for copy in small_copies:
        copy.wait()
    az_rows = tap_rows(az_frac[...], 256)
    rg_rows = tap_rows(rg_frac[...], 256)
    span = rows_n + 2 * RIM
    az_taps = band(az_rows[:, :span], iota((rows_n, span), 1) - iota((rows_n, span), 0) - (az_off[...] + RIM))
    rg_shape = (BLOCK + 2 * SIDE, BLOCK)
    rg_taps = band(rg_rows, iota(rg_shape, 0) - iota(rg_shape, 1) - (rg_off[...] + SIDE))
    azim[:, pl.ds(0, SIDE)] = jnp.zeros((2 * rows_n, SIDE), BF16)
    azim[:, pl.ds(SIDE + cols_n, SIDE)] = jnp.zeros((2 * rows_n, SIDE), BF16)
    lanes = iota((1, mask.shape[1]), 1)
    marks = jnp.where(mask[...] != 0, 1.0, 0.0).astype(F32)
    picked = iota((LAG, mask.shape[1]), 1) == iota((LAG, mask.shape[1]), 0) + (rows_n - LAG)
    weight = jnp.sum(jnp.where(picked, marks, 0.0), axis=1, keepdims=True)
    count = jnp.sum(marks, axis=1, keepdims=True) * float(cols_n)

    round_wait(0)
    round_signal(1)
    turn(1)
    turn(3)
    for k in range(1, NX):
        @pl.when(jnp.logical_not(x_first[k]))
        def _(k=k):
            pl.semaphore_wait(x_ready.at[k - 1], 1)
    spread_back(0, zh)

    def take_near():
        arrival(near)

        @pl.when(passes[0][0])
        def _():
            passes[0][1].start()

        spread(near, z_at(near))

    @pl.when(zh != 2)
    def _():
        take_near()

    own_copy.wait()

    @pl.when(t > 0)
    def _():
        up.wait_recv()

    @pl.when(t < tiles - 1)
    def _():
        down.wait_recv()

    for plane in range(2):
        for b in range(cols_n // BLOCK):
            part = jnp.dot(az_taps, ext[plane, :, pl.ds(b * BLOCK, BLOCK)], preferred_element_type=F32)
            azim[pl.ds(plane * rows_n, rows_n), pl.ds(SIDE + b * BLOCK, BLOCK)] = part.astype(BF16)


    round_wait(1)
    round_signal(2)
    def row_copy(plane, b):
        piece = pl.ds(b * (BLOCK // 128), BLOCK // 128)
        return remote(
            res.at[piece, pl.ds(plane * rows_n, LAG), :], rnext.at[plane, piece], row_send.at[plane, b], row_recv.at[plane, b],
            lax.rem(t + tiles - 1, tiles), d,
        )

    def send_rows(b):
        @pl.when(t > 0)
        def _():
            row_copy(0, b).start()
            row_copy(1, b).start()

    for b in range(cols_n // BLOCK):
        part = jnp.dot(azim[:, pl.ds(b * BLOCK, BLOCK + 2 * SIDE)], rg_taps, preferred_element_type=F32).astype(BF16)
        for h in range(BLOCK // 128):
            half = part[:, h * 128 : (h + 1) * 128]
            res[b * (BLOCK // 128) + h] = half
        if b > 0:
            send_rows(b - 1)
    send_rows(cols_n // BLOCK - 1)


    round_wait(2)
    round_signal(3)
    @pl.when(zh == 2)
    def _():
        take_near()

    round_wait(3)
    round_signal(4)
    arrival(far)

    @pl.when(passes[1][0])
    def _():
        passes[1][1].start()

    spread(far, z_at(far))
    arrival(2)
    spread(2, z_at(2))

    @pl.when(t < tiles - 1)
    def _():
        for b in range(cols_n // BLOCK):
            for plane in range(2):
                row_copy(plane, b).wait_recv()

    low_half = iota((rows_n, 128), 1) < width

    def product(block_of, z, q, r_re, r_im, low):
        a = block_of[z, 2 * q].astype(F32)
        b = block_of[z, 2 * q + 1].astype(F32)
        p_re = jnp.where(low, a, pltpu.roll(b, width, 1))
        p_im = jnp.where(low, pltpu.roll(a, width, 1), b)
        return p_re * r_re + p_im * r_im, p_im * r_re - p_re * r_im

    def fold(v):
        return jnp.sum(v.reshape(LAG // 8, 8, 128), axis=0)

    def beat(group, z, sums):
        for k in range(1, NX):
            x_copy(group, z, k).wait_recv()

        @pl.when(t < tiles - 1)
        def _():
            for k in range(NX):
                next_copy(group, z, k).wait_recv()

        e_re, e_im, power = sums
        for q in range(NX // 2):
            m = z * (NX // 2) + q
            i_re, i_im = product(
                gath, z, q, res[m, pl.ds(0, rows_n)].astype(F32), res[m, pl.ds(rows_n, rows_n)].astype(F32), low_half
            )
            ifg[m, pl.ds(0, rows_n)] = i_re
            ifg[m, pl.ds(rows_n, rows_n)] = i_im
            l_re, l_im = product(gnext, z, q, rnext[0, m].astype(F32), rnext[1, m].astype(F32), low_half[:LAG])
            a_re, a_im = i_re[rows_n - LAG :], i_im[rows_n - LAG :]
            e_re += fold(weight * (a_re * l_re + a_im * l_im))
            e_im += fold(weight * (a_im * l_re - a_re * l_im))
            power += fold((0.5 * weight) * (a_re * a_re + a_im * a_im + l_re * l_re + l_im * l_im))
        return e_re, e_im, power

    zeros = jnp.zeros((8, 128), F32)
    sums = beat(0, zh, (zeros, zeros, zeros))
    sums = beat(1, z_at(1), sums)
    sums = beat(3, z_at(3), sums)
    round_wait(4)
    sums = beat(2, z_at(2), sums)

    lane = iota((1, 128), 1)
    own = jnp.where(lane == 3, count, 0.0)
    for k, v in enumerate(sums):
        own = jnp.where(lane == k, jnp.sum(jnp.sum(v, axis=0, keepdims=True), axis=1, keepdims=True), own)
    stat_out[0] = own

    zl, y, core = t // 8, lax.rem(t // 2, 4), lax.rem(t, 2)
    offsets = [(dz, dy, dc) for dy in (2, 1, 3, 0) for dz in (3, 1, 2, 0) for dc in (1, 0)][: tiles - 1]

    def stat_copy(i):
        dz, dy, dc = offsets[i]
        tile = lax.rem(zl + dz, 4) * 8 + lax.rem(y + dy, 4) * 2 + lax.rem(core + dc, 2)
        return remote(stat_out, stat_in.at[pl.ds(i, 1)], stat_send, stat_recv, tile, d)

    for i in range(tiles - 1):
        stat_copy(i).start()

    total = jnp.zeros((2 * rows_n, 128), F32)
    per = 128 // LR
    for m in range(chunks):
        pick = jnp.where(iota((128, 128), 1) == m * per + iota((128, 128), 0) // LR, 1.0 / (LA * LR), 0.0).astype(BF16)
        v = ifg[m]
        hi = v.astype(BF16)
        lo = (v - hi.astype(F32)).astype(BF16)
        total += jnp.dot(hi, pick, preferred_element_type=F32) + jnp.dot(lo, pick, preferred_element_type=F32)
    acc[...] = total
    pairs = [acc[pl.ds(first, rows_n, stride=LA), :] for first in range(LA)]
    both = functools.reduce(lambda a, b: a + b, pairs)
    looks_re, looks_im = both[: rows_n // LA], both[rows_n // LA :]

    pltpu.make_async_copy(stat_in, stat_in, stat_recv).wait()
    grand = own + jnp.sum(stat_in[...], axis=0)
    t_re, t_im, t_pow, t_cnt = (jnp.sum(jnp.where(lane == k, grand, 0.0), axis=1, keepdims=True) for k in range(4))
    magnitude = jnp.sqrt(t_re * t_re + t_im * t_im)
    floor_val = (t_pow + 1e-06) / jnp.sqrt(jnp.maximum(t_cnt, 1.0))
    denom = jnp.maximum(magnitude, floor_val)
    u_re = t_re / denom
    u_im = t_im / denom
    out[0, 0] = looks_re * u_re + looks_im * u_im
    out[0, 1] = looks_im * u_re - looks_re * u_im

    for copy in z_copies.values():
        copy.wait_send()

    @pl.when(zh == 2)
    def _():
        direct.wait_send()

    for here, copy in passes:
        @pl.when(here)
        def _(copy=copy):
            copy.wait_send()
    for group in range(nz):
        for k in range(1, NX):
            x_copy(group, z_at(group), k).wait_send()

    @pl.when(t < tiles - 1)
    def _():
        up.wait_send()

    @pl.when(t > 0)
    def _():
        down.wait_send()
        for group in range(nz):
            for k in range(NX):
                next_copy(group, z_at(group), k).wait_send()
        for b in range(cols_n // BLOCK):
            for plane in range(2):
                row_copy(plane, b).wait_send()

    pltpu.make_async_copy(stat_in, stat_in, stat_send).wait()


def solution(mesh):
    tiles, dates = mesh.shape["tile"], mesh.shape["date"]
    nz = dates // NX

    def shards(secondary, primary, margin_mask, az_off, rg_off, az_frac, rg_frac):
        rows_n, cols_n = secondary.shape[2:]
        width = primary.shape[2]
        hbm = pl.BlockSpec(memory_space=pltpu.HBM)
        vmem = pl.BlockSpec(memory_space=pltpu.VMEM)
        dma = pltpu.SemaphoreType.DMA
        regular = pltpu.SemaphoreType.REGULAR
        chunks = cols_n // 128
        return pl.pallas_call(
            functools.partial(kernel, tiles, dates),
            out_shape=pltpu.VMEM((1, 2, rows_n // LA, cols_n // LR), F32),
            in_specs=[hbm] * 7,
            out_specs=vmem,
            scratch_shapes=[
                pltpu.VMEM((1, rows_n), jnp.int32),
                *[pltpu.VMEM((1, 1), jnp.int32)] * 2,
                *[pltpu.VMEM((1, 1), F32)] * 2,
                pltpu.VMEM((2, rows_n + 2 * RIM, cols_n), BF16),
                pltpu.VMEM((2 * width, rows_n), BF16),
                pltpu.VMEM((2 * rows_n, cols_n + 2 * SIDE), BF16),
                pltpu.VMEM((nz, NX, rows_n, 2 * width), BF16),
                pltpu.VMEM((chunks, 2 * rows_n, 128), BF16),
                pltpu.VMEM((chunks, 2 * rows_n, 128), F32),
                pltpu.VMEM((nz, NX, LAG, 2 * width), BF16),
                pltpu.VMEM((2, chunks, LAG, 128), BF16),
                pltpu.VMEM((1, 1, 128), F32),
                pltpu.VMEM((tiles - 1, 1, 128), F32),
                pltpu.VMEM((2 * rows_n, 128), F32),
                dma((7,)), dma((2,)), dma((2,)), dma((4,)), dma((3,)),
                dma((nz, NX - 1)), dma((nz, NX - 1)), dma((nz, NX)), dma((nz, NX)), dma((2, cols_n // BLOCK)), dma((2, cols_n // BLOCK)), dma, dma,
                regular((nz - 1,)), regular((NX - 1,)), regular, regular((len(ROUNDS),)),
            ],
            compiler_params=pltpu.CompilerParams(collective_id=0, has_side_effects=True),
            name="coregister",
        )(secondary, primary.transpose(0, 2, 1).reshape(2 * width, rows_n), margin_mask.reshape(1, rows_n), az_off, rg_off, az_frac, rg_frac)

    return jax.shard_map(
        shards,
        mesh=mesh,
        in_specs=(
            P("date", None, "tile", None),
            P(None, "tile", "date"),
            P("tile"),
            P("date", "tile"),
            P("date", "tile"),
            P("date", "tile"),
            P("date", "tile"),
        ),
        out_specs=P("date", None, "tile", None),
        check_vma=False,
    )
```
